32 devices in a mesh: groups: 2 (over y), assets: 8 (over z, x), tm: 2 (over core).
Axes of the slice: x: 2, y: 2, z: 4, core: 2. Of those that a mesh axis runs over, the one named last changes fastest.
Arguments:
- returns: bfloat16 [1536, 16384], P('tm', ('groups', 'assets')), parts along dimension 1, may hold values from -24 to 24
- prior: float32 [16384, 8192], P(('groups', 'assets')), parts along dimension 0, may hold values from -3 to 3
Outputs:
- covariance: float32 [2, 16384, 8192], P('tm', ('groups', 'assets')), parts along dimension 1
The draws below stay inside these ranges and needn't reach their ends.
There are 2 independent parts, one for each index of `groups`. The reference program is written for one: setup_inputs(seed, part) draws one part's arguments, and reference() takes and returns one part's arrays. A program takes and returns all parts, laid end to end along the dimension named above; each array names one. Nothing has to cross between parts.
All inputs are finite; a program needn't handle non-finite values.
Results may differ from the reference program's by a relative error of at most 0.0045.
Values may be sent and summed in bfloat16 or wider, within the bound.
No kernel may reach another device: no remote copies, remote signals or barrier semaphores. Data moves between devices by JAX's collectives and lax.ppermute only.
A program may use at most 256 MiB of HBM per device.

```python
import jax
import jax.numpy as jnp
from jax import lax

ASSETS = 8192
MIN_DEV = 768
SLABS = 2
MINUTES = 1536


def block_levels(stream_key, dims, cuts, smallest, top_value):
    factor_of = 1.0
    for dim, blocks in cuts:
        steps = jax.random.uniform(jax.random.fold_in(jax.random.fold_in(stream_key, 6), dim), (blocks,), jnp.float32, smallest / len(cuts), top_value / len(cuts))
        factor_of = factor_of * jnp.repeat(jnp.exp(steps), dims[dim] // blocks).reshape((-1,) + (1,) * (len(dims) - 1 - dim))
    return factor_of


def scatter_about(stream_key, extent, width, reach, shards=(), held_as=jnp.bfloat16):
    drawn = jax.random.normal(stream_key, extent, jnp.float32) * width
    if len(shards) > 0:
        drawn = block_levels(stream_key, extent, shards, -0.22, 0.18) * drawn
    return jnp.clip(drawn, min=-reach, max=reach).astype(held_as)


def setup_inputs(seed: int = 0, part: int = 0) -> dict:
    streams_of = jax.random.split(jax.random.key(seed), 3)
    own_keys = jax.random.split(jax.random.fold_in(streams_of[2], part), 3)
    returns = scatter_about(own_keys[0], (MINUTES, ASSETS), 4.0, 24.0, ((0, 2), (1, 8)))
    prior = scatter_about(own_keys[1], (ASSETS, ASSETS), 0.5, 3.0, ((0, 8),), jnp.float32)
    return dict(returns=returns, prior=prior)


def reference(returns, prior):
    lam = jnp.float32(0.9995)
    position = jnp.arange(MIN_DEV, dtype=jnp.float32)
    weight = jnp.sqrt((jnp.float32(1.0) - lam) * jnp.power(lam, jnp.float32(MIN_DEV - 1) - position))
    factor = jnp.power(lam, jnp.float32(MIN_DEV))
    carry = prior
    results = []
    for slab in range(SLABS):
        piece = returns[slab * MIN_DEV:(slab + 1) * MIN_DEV]
        scaled = (piece.astype(jnp.float32) * weight[:, None]).astype(jnp.bfloat16).astype(jnp.float32)
        gram = jnp.dot(scaled.T, scaled, precision=lax.Precision.HIGHEST)
        carry = factor * carry + gram
        results.append(carry)
    return jnp.stack(results)
```

```python
import functools

import jax
import jax.numpy as jnp
from jax import lax
from jax.experimental import pallas as pl
from jax.experimental.pallas import tpu as pltpu
from jax.sharding import PartitionSpec as P

LANES = 128


def weights(minutes):
    lam = jnp.float32(0.9995)
    position = jnp.arange(minutes, dtype=jnp.float32)
    weight = jnp.sqrt(
        (jnp.float32(1.0) - lam) * jnp.power(lam, jnp.float32(minutes - 1) - position)
    )
    return weight, jnp.power(lam, jnp.float32(minutes))


def scale(part, weight):
    return (part.astype(jnp.float32) * weight[:, None]).astype(jnp.bfloat16)


def prefix(shard, axis, combine, identity):
    length, mine = (lax.axis_size(axis), lax.axis_index(axis))
    everything = jax.tree.map(
        lambda part: lax.all_gather(part.astype(jnp.bfloat16), axis), shard
    )
    start = jax.tree.map(
        lambda part, zero: jnp.broadcast_to(jnp.asarray(zero, part.dtype), part.shape),
        shard,
        identity,
    )

    def turn(k, before):
        reached = k < mine
        new = combine(
            before, jax.tree.map(lambda part, own: part[k].astype(own.dtype), everything, shard)
        )
        return jax.tree.map(lambda a, b: jnp.where(reached, a, b), new, before)

    return lax.fori_loop(0, length, turn, start)


def combine_carry(earlier, later):
    return (later[1] * earlier[0] + later[0], earlier[1] * later[1])


def local_any(returns, prior):
    weight, factor = weights(returns.shape[0])
    scaled = scale(returns, weight)
    tile = lax.dot_general(
        scaled,
        lax.all_gather(scaled, "assets", axis=1, tiled=True),
        (((0,), (0,)), ((), ())),
        preferred_element_type=jnp.float32,
    )
    decay = jnp.full((1,), factor, jnp.float32)
    identity = (jnp.zeros_like(tile), jnp.ones((1,), jnp.float32))
    before, reach = prefix((tile, decay), "tm", combine_carry, identity)
    return (factor * (before + reach[0] * prior) + tile)[None]


def tile_kernel(count, columns, coef, *refs):
    own = refs[:count]
    other = refs[count : 2 * count]
    weight, left_own, left_other, prior = refs[2 * count : 2 * count + 4]
    out, rhs_own, rhs_other = refs[-3:]
    width = rhs_own.shape[1]
    earlier = coef[1] != 0.0

    def scaled(source, target):
        for lane in range(0, width, LANES):
            at = slice(lane, lane + LANES)
            target[:, at] = (source[:, at].astype(jnp.float32) * weight[...]).astype(jnp.bfloat16)

    piece = pl.program_id(0)

    @pl.when(pl.program_id(1) == 0)
    def _():
        for k in range(count):

            @pl.when(piece == k)
            def _():
                scaled(own[k], rhs_own)

                @pl.when(earlier)
                def _():
                    scaled(other[k], rhs_other)

    base = coef[0] * prior[...] + jnp.dot(
        left_own[...], rhs_own[...], preferred_element_type=jnp.float32
    )

    @pl.when(earlier)
    def _():
        out[0] = base + coef[1] * jnp.dot(
            left_other[...], rhs_other[...], preferred_element_type=jnp.float32
        )

    @pl.when(jnp.logical_not(earlier))
    def _():
        out[0] = base


def turn_kernel(count, *refs):
    weight, out = refs[count], refs[-1]
    for k in range(count):

        @pl.when(pl.program_id(0) == k)
        def _():
            for lane in range(0, refs[k].shape[1], LANES):
                part = refs[k][:, lane : lane + LANES].astype(jnp.float32) * weight[...]
                out[lane : lane + LANES, :] = part.T.astype(jnp.bfloat16)


def turn_call(pieces, weight):
    count = len(pieces)
    minutes, width = pieces[0].shape
    return pl.pallas_call(
        functools.partial(turn_kernel, count),
        out_shape=jax.ShapeDtypeStruct((count * width, minutes), jnp.bfloat16),
        grid=(count,),
        in_specs=[pl.BlockSpec((minutes, width), lambda k: (0, 0))] * count
        + [pl.BlockSpec((minutes, LANES), lambda k: (0, 0))],
        out_specs=pl.BlockSpec((width, minutes), lambda k: (k, 0)),
        cost_estimate=pl.CostEstimate(
            flops=count * minutes * width,
            bytes_accessed=4 * count * minutes * width,
            transcendentals=0,
        ),
    )(*pieces, weight)


def tile_call(out, columns, coef, own, other, weight, left_own, left_other, prior, rows):
    count = len(own)
    minutes, width = own[0].shape
    height, total = prior.shape
    whole = lambda: pl.BlockSpec((minutes, width), lambda k, i, *_: (0, 0))
    in_specs = (
        [whole() for _ in range(2 * count)]
        + [pl.BlockSpec((minutes, LANES), lambda k, i, *_: (0, 0))]
        + [pl.BlockSpec((rows, minutes), lambda k, i, *_: (i, 0))] * 2
        + [pl.BlockSpec((rows, width), lambda k, i, columns, coef: (i, columns[k]))]
    )
    args = [*own, *other, weight, left_own, left_other, prior]
    aliases = {}
    if out is not None:
        in_specs.append(pl.BlockSpec(memory_space=pl.ANY))
        aliases = {2 + len(args): 0}
        args.append(out)
    flops = 4 * count * minutes * width * height
    return pl.pallas_call(
        functools.partial(tile_kernel, count),
        out_shape=jax.ShapeDtypeStruct((1, height, total), jnp.float32),
        grid_spec=pltpu.PrefetchScalarGridSpec(
            num_scalar_prefetch=2,
            grid=(count, height // rows),
            in_specs=in_specs,
            out_specs=pl.BlockSpec(
                (1, rows, width), lambda k, i, columns, coef: (0, i, columns[k])
            ),
            scratch_shapes=[pltpu.VMEM((minutes, width), jnp.bfloat16)] * 2,
        ),
        input_output_aliases=aliases,
        compiler_params=pltpu.CompilerParams(dimension_semantics=("arbitrary", "arbitrary")),
        cost_estimate=pl.CostEstimate(
            flops=flops,
            bytes_accessed=count * (8 * width * height + 4 * width * minutes)
            + 4 * height * minutes,
            transcendentals=0,
        ),
    )(columns, coef, *args)


def local_ring(returns, prior):
    minutes, width = returns.shape
    height, total = prior.shape
    n = lax.axis_size("assets")
    me, slab = lax.axis_index("assets"), lax.axis_index("tm")
    half = width // 2
    rows = min(height, 256)

    cycle = list(range(0, n, 2)) + list(range(n - 1, 0, -2))
    forward = [(cycle[k], cycle[(k + 1) % n]) for k in range(n)]
    backward = [(b, a) for a, b in forward]
    place = jnp.where(me % 2 == 0, me // 2, n - 1 - me // 2)

    def owner(step):
        at = lax.rem(place - step + 2 * n, n)
        return jnp.where(at < n // 2, 2 * at, 2 * (n - 1 - at) + 1)

    swap = lambda part: lax.ppermute(part, "tm", [(0, 1), (1, 0)])

    weight, factor = weights(minutes)
    wide = jnp.broadcast_to(weight[:, None], (minutes, LANES))
    coef = jnp.where(slab == 0, jnp.stack([factor, 0.0]), jnp.stack([factor * factor, factor]))

    halves = [returns[:, :half], returns[:, half:]]
    flight = {(0, h): halves[h] for h in (0, 1)} | {(1, h): halves[h] for h in (0, 1)}
    slots = []
    for k in range(n - 1):
        pair = []
        for way, pairs in ((0, forward), (1, backward)):
            h = (k + way) % 2
            flight[way, h] = lax.ppermute(flight[way, h], "assets", pairs)
            pair.append(flight[way, h])
        slots.append(pair)

    own_other = [swap(h) for h in halves]
    left_own = turn_call(halves, wide)
    left_other = turn_call(own_other, wide)

    common = (wide, left_own, left_other, prior, rows)
    columns = 2 * me + jnp.arange(2, dtype=jnp.int32)
    out = tile_call(None, columns, coef, halves, own_other, *common)
    for k, pair in enumerate(slots):
        step = k // 2 + 1
        h = k % 2
        side = jnp.array([step, -step], jnp.int32)
        columns = 2 * owner(side) + jnp.array([h, 1 - h], jnp.int32)
        out = tile_call(out, columns, coef, pair, [swap(p) for p in pair], *common)
    return out


def solution(mesh):
    width_lanes = 4 * LANES

    def local(returns, prior):
        n, slabs = lax.axis_size("assets"), lax.axis_size("tm")
        ring = slabs == 2 and n % 2 == 0 and n <= 16 and returns.shape[1] % width_lanes == 0
        return (local_ring if ring else local_any)(returns, prior)

    placed = (P("tm", ("groups", "assets")), P(("groups", "assets"), None))
    return jax.shard_map(
        local,
        mesh=mesh,
        in_specs=placed,
        out_specs=P("tm", ("groups", "assets"), None),
        check_vma=False,
    )
```

```python
import functools

import jax
import jax.numpy as jnp
from jax import lax
from jax.experimental import pallas as pl
from jax.experimental.pallas import tpu as pltpu
from jax.sharding import PartitionSpec as P


LANES = 128


def weights(minutes):
    lam = jnp.float32(0.9995)
    position = jnp.arange(minutes, dtype=jnp.float32)
    weight = jnp.sqrt(
        (jnp.float32(1.0) - lam) * jnp.power(lam, jnp.float32(minutes - 1) - position)
    )
    return weight, jnp.power(lam, jnp.float32(minutes))


def scale(part, weight):
    return (part.astype(jnp.float32) * weight[:, None]).astype(jnp.bfloat16)


def prefix(shard, axis, combine, identity):
    length, mine = (lax.axis_size(axis), lax.axis_index(axis))
    everything = jax.tree.map(
        lambda part: lax.all_gather(part.astype(jnp.bfloat16), axis), shard
    )
    start = jax.tree.map(
        lambda part, zero: jnp.broadcast_to(jnp.asarray(zero, part.dtype), part.shape),
        shard,
        identity,
    )

    def turn(k, before):
        reached = k < mine
        new = combine(
            before, jax.tree.map(lambda part, own: part[k].astype(own.dtype), everything, shard)
        )
        return jax.tree.map(lambda a, b: jnp.where(reached, a, b), new, before)

    return lax.fori_loop(0, length, turn, start)


def combine_carry(earlier, later):
    return (later[1] * earlier[0] + later[0], earlier[1] * later[1])


def local_any(returns, prior):
    weight, factor = weights(returns.shape[0])
    scaled = scale(returns, weight)
    tile = lax.dot_general(
        scaled,
        lax.all_gather(scaled, "assets", axis=1, tiled=True),
        (((0,), (0,)), ((), ())),
        preferred_element_type=jnp.float32,
    )
    decay = jnp.full((1,), factor, jnp.float32)
    identity = (jnp.zeros_like(tile), jnp.ones((1,), jnp.float32))
    before, reach = prefix((tile, decay), "tm", combine_carry, identity)
    return (factor * (before + reach[0] * prior) + tile)[None]


def tile_kernel(count, rows, columns, coef, *refs):
    own, other = refs[:count], refs[count : 2 * count]
    weight, left_own, left_other, prior = refs[2 * count : 2 * count + 4]
    out, x_own, x_other, box, x_sem, in_sem, out_sem = refs[-7:]
    width = own[0].shape[1]
    tiles = prior.shape[0] // rows
    earlier = coef[1] != 0.0
    copy = pltpu.make_async_copy

    def place(k):
        return pl.ds(pl.multiple_of(columns[k] * LANES, LANES), width)

    def inside(k):
        return pl.ds(k * width, width)

    def take(part, x, side, k):
        return copy(part[k], x.at[:, inside(k)], x_sem.at[side, k])

    def fetch(k, i):
        at = pl.ds(i * rows, rows)
        return copy(prior.at[at, place(k)], box.at[at, inside(k)], in_sem.at[k, i])

    def flush(k, i):
        at = pl.ds(i * rows, rows)
        return copy(box.at[at, inside(k)], out.at[0, at, place(k)], out_sem.at[k, i])

    def scale_in_place(ref, k):
        for lane in range(k * width, (k + 1) * width, LANES):
            at = slice(lane, lane + LANES)
            ref[:, at] = (ref[:, at].astype(jnp.float32) * weight[...]).astype(jnp.bfloat16)

    for k in range(count):
        take(own, x_own, 0, k).start()

        @pl.when(earlier)
        def _():
            take(other, x_other, 1, k).start()

    for i in range(tiles):
        for k in range(count):
            fetch(k, i).start()

    for k in range(count):
        take(own, x_own, 0, k).wait()
        scale_in_place(x_own, k)

        @pl.when(earlier)
        def _():
            take(other, x_other, 1, k).wait()
            scale_in_place(x_other, k)

    @pl.loop(0, tiles)
    def _(i):
        at = pl.ds(pl.multiple_of(i * rows, rows), rows)
        for k in range(count):
            fetch(k, i).wait()
        base = coef[0] * box[at] + jnp.dot(
            left_own[at], x_own[...], preferred_element_type=jnp.float32
        )

        @pl.when(earlier)
        def _():
            box[at] = base + coef[1] * jnp.dot(
                left_other[at], x_other[...], preferred_element_type=jnp.float32
            )

        @pl.when(jnp.logical_not(earlier))
        def _():
            box[at] = base

        for k in range(count):
            flush(k, i).start()

    for i in range(tiles):
        for k in range(count):
            flush(k, i).wait()


def turn_kernel(count, *refs):
    weight, out = refs[count], refs[-1]
    for k in range(count):

        @pl.when(pl.program_id(0) == k)
        def _():
            for lane in range(0, refs[k].shape[1], LANES):
                part = refs[k][:, lane : lane + LANES].astype(jnp.float32) * weight[...]
                out[lane : lane + LANES, :] = part.T.astype(jnp.bfloat16)


def turn_call(pieces, weight):
    count = len(pieces)
    minutes, width = pieces[0].shape
    return pl.pallas_call(
        functools.partial(turn_kernel, count),
        out_shape=jax.ShapeDtypeStruct((count * width, minutes), jnp.bfloat16),
        grid=(count,),
        in_specs=[pl.BlockSpec((minutes, width), lambda k: (0, 0))] * count
        + [pl.BlockSpec((minutes, LANES), lambda k: (0, 0))],
        out_specs=pl.BlockSpec((width, minutes), lambda k: (k, 0)),
        cost_estimate=pl.CostEstimate(
            flops=count * minutes * width,
            bytes_accessed=4 * count * minutes * width,
            transcendentals=0,
        ),
    )(*pieces, weight)


def tile_call(out, columns, coef, own, other, weight, left_own, left_other, prior, rows):
    count = len(own)
    minutes, width = own[0].shape
    height, total = prior.shape
    tiles = height // rows
    near = pl.BlockSpec(memory_space=pltpu.VMEM)
    far = pl.BlockSpec(memory_space=pl.ANY)
    scalar = pl.BlockSpec(memory_space=pltpu.SMEM)
    args = [columns, coef, *own, *other, weight, left_own, left_other, prior]
    in_specs = [scalar] * 2 + [far] * (2 * count) + [near] * 3 + [far]
    aliases = {}
    if out is not None:
        aliases = {len(args): 0}
        in_specs.append(far)
        args.append(out)
    return pl.pallas_call(
        functools.partial(tile_kernel, count, rows),
        out_shape=jax.ShapeDtypeStruct((1, height, total), jnp.float32),
        in_specs=in_specs,
        out_specs=far,
        scratch_shapes=[
            pltpu.VMEM((minutes, count * width), jnp.bfloat16),
            pltpu.VMEM((minutes, count * width), jnp.bfloat16),
            pltpu.VMEM((height, count * width), jnp.float32),
            pltpu.SemaphoreType.DMA((2, count)),
            pltpu.SemaphoreType.DMA((count, tiles)),
            pltpu.SemaphoreType.DMA((count, tiles)),
        ],
        input_output_aliases=aliases,
        compiler_params=pltpu.CompilerParams(vmem_limit_bytes=24 * 2**20),
        cost_estimate=pl.CostEstimate(
            flops=4 * count * minutes * width * height,
            bytes_accessed=count * (8 * width * height + 4 * width * minutes),
            transcendentals=0,
        ),
    )(*args)


def last_cuts(half):
    return (half // 2, half // 4, half // 4)


def local_ring(returns, prior):
    minutes, width = returns.shape
    n = lax.axis_size("assets")
    me, slab = lax.axis_index("assets"), lax.axis_index("tm")
    half = width // 2
    rows = min(prior.shape[0], 512)

    cycle = list(range(0, n, 2)) + list(range(n - 1, 0, -2))
    forward = [(cycle[k], cycle[(k + 1) % n]) for k in range(n)]
    backward = [(b, a) for a, b in forward]
    place = jnp.where(me % 2 == 0, me // 2, n - 1 - me // 2)

    def owner(step):
        at = lax.rem(place - step + 2 * n, n)
        return jnp.where(at < n // 2, 2 * at, 2 * (n - 1 - at) + 1)

    def swap(pieces):
        moved = []
        for part in pieces:
            moved.append(lax.ppermute(part, "tm", [(0, 1), (1, 0)]))
        return moved

    weight, factor = weights(minutes)
    wide = jnp.broadcast_to(weight[:, None], (minutes, LANES))
    coef = jnp.where(slab == 0, jnp.stack([factor, 0.0]), jnp.stack([factor * factor, factor]))

    def hop(parts):
        moved = []
        for way, pairs in enumerate((forward, backward)):
            moved.append(lax.ppermute(parts[way], "assets", pairs))
        return moved

    halves = [returns[:, :half], returns[:, half:]]
    flight = [halves, halves[::-1]]
    arrived = []
    for k in range(n - 2):
        flight[k % 2] = hop(flight[k % 2])
        arrived.append((flight[k % 2], k // 2 + 1, (k % 2, 1 - k % 2), 0))
    start = 0
    for part in last_cuts(half):
        cut = slice(start, start + part)
        arrived.append((hop([f[:, cut] for f in flight[0]]), n // 2, (0, 1), start))
        start = start + part

    own_other = swap(halves)
    left_own = turn_call(halves, wide)
    left_other = turn_call(own_other, wide)

    common = (wide, left_own, left_other, prior, rows)
    unit = half // LANES
    columns = (2 * me + jnp.arange(2, dtype=jnp.int32)) * unit
    out = tile_call(None, columns, coef, halves, own_other, *common)
    for pair, step, sides, start in arrived:
        block = owner(jnp.array([step, -step], jnp.int32))
        columns = (2 * block + jnp.array(sides, jnp.int32)) * unit + start // LANES
        other = swap(pair)
        out = tile_call(out, columns, coef, pair, other, *common)
    return out


def solution(mesh):
    n, slabs = mesh.shape["assets"], mesh.shape["tm"]

    def rings(width):
        return slabs == 2 and n % 2 == 0 and 4 <= n <= 16 and width % (8 * LANES) == 0

    def local(returns, prior):
        if not rings(returns.shape[1]):
            return local_any(returns, prior)
        return local_ring(returns, prior)

    placed = (P("tm", ("groups", "assets")), P(("groups", "assets"), None))
    return jax.shard_map(
        local,
        mesh=mesh,
        in_specs=placed,
        out_specs=P("tm", ("groups", "assets"), None),
        check_vma=False,
    )
```

```python
import functools

import jax
import jax.numpy as jnp
from jax import lax
from jax.experimental import pallas as pl
from jax.experimental.pallas import tpu as pltpu
from jax.sharding import PartitionSpec as P


LANES = 128
LAST_HOPS = 2


def weights(minutes):
    lam = jnp.float32(0.9995)
    position = jnp.arange(minutes, dtype=jnp.float32)
    weight = jnp.sqrt(
        (jnp.float32(1.0) - lam) * jnp.power(lam, jnp.float32(minutes - 1) - position)
    )
    return weight, jnp.power(lam, jnp.float32(minutes))


def scale(part, weight):
    return (part.astype(jnp.float32) * weight[:, None]).astype(jnp.bfloat16)


def prefix(shard, axis, combine, identity):
    length, mine = (lax.axis_size(axis), lax.axis_index(axis))
    everything = jax.tree.map(
        lambda part: lax.all_gather(part.astype(jnp.bfloat16), axis), shard
    )
    start = jax.tree.map(
        lambda part, zero: jnp.broadcast_to(jnp.asarray(zero, part.dtype), part.shape),
        shard,
        identity,
    )

    def turn(k, before):
        reached = k < mine
        new = combine(
            before, jax.tree.map(lambda part, own: part[k].astype(own.dtype), everything, shard)
        )
        return jax.tree.map(lambda a, b: jnp.where(reached, a, b), new, before)

    return lax.fori_loop(0, length, turn, start)


def combine_carry(earlier, later):
    return (later[1] * earlier[0] + later[0], earlier[1] * later[1])


def local_any(returns, prior):
    weight, factor = weights(returns.shape[0])
    scaled = scale(returns, weight)
    tile = lax.dot_general(
        scaled,
        lax.all_gather(scaled, "assets", axis=1, tiled=True),
        (((0,), (0,)), ((), ())),
        preferred_element_type=jnp.float32,
    )
    decay = jnp.full((1,), factor, jnp.float32)
    identity = (jnp.zeros_like(tile), jnp.ones((1,), jnp.float32))
    before, reach = prefix((tile, decay), "tm", combine_carry, identity)
    return (factor * (before + reach[0] * prior) + tile)[None]


def tile_kernel(count, group, rows, columns, coef, *refs):
    own, other = refs[:count], refs[count : 2 * count]
    weight, left_own, left_other, prior = refs[2 * count : 2 * count + 4]
    out, box, rhs, in_sem, out_sem = refs[-5:]
    width = own[0].shape[1]
    height = prior.shape[0]
    earlier = coef[1] != 0.0
    copy = pltpu.make_async_copy
    joined = width < group
    turns = 1 if joined else count * (width // group)
    part = width if joined else group
    parts = count if joined else 1

    def where(turn, j):
        if joined:
            return j, 0
        return turn // (width // group), (turn % (width // group)) * group

    def place(turn, j):
        k, start = where(turn, j)
        return pl.ds(pl.multiple_of(columns[k] * LANES + start, part), part)

    def fetch(turn, j):
        at = pl.ds(j * part, part)
        return copy(prior.at[:, place(turn, j)], box.at[turn, :, at], in_sem.at[turn, j])

    def flush(turn, j, i):
        at, down = pl.ds(j * part, part), pl.ds(i * rows, rows)
        return copy(
            box.at[turn, down, at], out.at[0, down, place(turn, j)], out_sem.at[turn, j, i]
        )

    def scaled(source, turn, j):
        k, start = where(turn, j)
        parts = [
            (source[k][:, start + lane : start + lane + LANES].astype(jnp.float32) * weight[...])
            .astype(jnp.bfloat16)
            for lane in range(0, part, LANES)
        ]
        return parts

    for turn in range(turns):
        for j in range(parts):
            fetch(turn, j).start()

    for turn in range(turns):
        for j in range(parts):
            for lane, piece in enumerate(scaled(own, turn, j)):
                rhs[0, :, j * part + lane * LANES : j * part + (lane + 1) * LANES] = piece

        @pl.when(earlier)
        def _():
            for j in range(parts):
                for lane, piece in enumerate(scaled(other, turn, j)):
                    rhs[1, :, j * part + lane * LANES : j * part + (lane + 1) * LANES] = piece

        for j in range(parts):
            fetch(turn, j).wait()

        @pl.loop(0, height // rows)
        def _(i):
            at = pl.ds(pl.multiple_of(i * rows, rows), rows)
            base = coef[0] * box[turn, at] + jnp.dot(
                left_own[at], rhs[0], preferred_element_type=jnp.float32
            )

            @pl.when(earlier)
            def _():
                box[turn, at] = base + coef[1] * jnp.dot(
                    left_other[at], rhs[1], preferred_element_type=jnp.float32
                )

            @pl.when(jnp.logical_not(earlier))
            def _():
                box[turn, at] = base

            for j in range(parts):
                flush(turn, j, i).start()

    for turn in range(turns):
        for j in range(parts):
            for i in range(height // rows):
                flush(turn, j, i).wait()


def turn_kernel(count, *refs):
    weight, out = refs[count], refs[-1]
    for k in range(count):

        @pl.when(pl.program_id(0) == k)
        def _():
            for lane in range(0, refs[k].shape[1], LANES):
                part = refs[k][:, lane : lane + LANES].astype(jnp.float32) * weight[...]
                out[lane : lane + LANES, :] = part.T.astype(jnp.bfloat16)


def turn_call(pieces, weight):
    count = len(pieces)
    minutes, width = pieces[0].shape
    return pl.pallas_call(
        functools.partial(turn_kernel, count),
        out_shape=jax.ShapeDtypeStruct((count * width, minutes), jnp.bfloat16),
        grid=(count,),
        in_specs=[pl.BlockSpec((minutes, width), lambda k: (0, 0))] * count
        + [pl.BlockSpec((minutes, LANES), lambda k: (0, 0))],
        out_specs=pl.BlockSpec((width, minutes), lambda k: (k, 0)),
        compiler_params=pltpu.CompilerParams(vmem_limit_bytes=34 * 2**20),
        cost_estimate=pl.CostEstimate(
            flops=count * minutes * width,
            bytes_accessed=4 * count * minutes * width,
            transcendentals=0,
        ),
    )(*pieces, weight)


def tile_call(out, columns, coef, own, other, weight, left_own, left_other, prior, rows, group):
    count = len(own)
    minutes, width = own[0].shape
    height, total = prior.shape
    group = min(group, count * width)
    turns, parts = max(1, count * width // group), (count if width < group else 1)
    near = pl.BlockSpec(memory_space=pltpu.VMEM)
    far = pl.BlockSpec(memory_space=pltpu.HBM)
    scalar = pl.BlockSpec(memory_space=pltpu.SMEM)
    args = [columns, coef, *own, *other, weight, left_own, left_other, prior]
    in_specs = [scalar] * 2 + [near] * (2 * count + 3) + [far]
    aliases = {}
    if out is not None:
        aliases = {len(args): 0}
        in_specs.append(far)
        args.append(out)
    return pl.pallas_call(
        functools.partial(tile_kernel, count, group, rows),
        out_shape=jax.ShapeDtypeStruct((1, height, total), jnp.float32),
        in_specs=in_specs,
        out_specs=far,
        scratch_shapes=[
            pltpu.VMEM((turns, height, group), jnp.float32),
            pltpu.VMEM((2, minutes, group), jnp.bfloat16),
            pltpu.SemaphoreType.DMA((turns, parts)),
            pltpu.SemaphoreType.DMA((turns, parts, height // rows)),
        ],
        input_output_aliases=aliases,
        compiler_params=pltpu.CompilerParams(vmem_limit_bytes=34 * 2**20),
        cost_estimate=pl.CostEstimate(
            flops=4 * count * minutes * width * height,
            bytes_accessed=count * (8 * width * height + 4 * width * minutes),
            transcendentals=0,
        ),
    )(*args)


def last_cuts(half):
    return (half // LAST_HOPS,) * LAST_HOPS


def local_ring(returns, prior):
    minutes, width = returns.shape
    n = lax.axis_size("assets")
    me, slab = lax.axis_index("assets"), lax.axis_index("tm")
    half = width // 2
    rows = min(prior.shape[0], 512)

    cycle = list(range(0, n, 2)) + list(range(n - 1, 0, -2))
    forward = [(cycle[k], cycle[(k + 1) % n]) for k in range(n)]
    backward = [(b, a) for a, b in forward]
    place = jnp.where(me % 2 == 0, me // 2, n - 1 - me // 2)

    def owner(step):
        at = lax.rem(place - step + 2 * n, n)
        return jnp.where(at < n // 2, 2 * at, 2 * (n - 1 - at) + 1)

    def swap(pieces):
        moved = []
        for part in pieces:
            moved.append(lax.ppermute(part, "tm", [(0, 1), (1, 0)]))
        return moved

    weight, factor = weights(minutes)
    wide = jnp.broadcast_to(weight[:, None], (minutes, LANES))
    coef = jnp.where(slab == 0, jnp.stack([factor, 0.0]), jnp.stack([factor * factor, factor]))

    def hop(parts):
        moved = []
        for way, pairs in enumerate((forward, backward)):
            moved.append(lax.ppermute(parts[way], "assets", pairs))
        return moved

    halves = [returns[:, :half], returns[:, half:]]
    flight = [halves, halves[::-1]]
    arrived = []
    for k in range(n - 2):
        flight[k % 2] = hop(flight[k % 2])
        arrived.append((flight[k % 2], k // 2 + 1, (k % 2, 1 - k % 2), 0))
    start = 0
    for part in last_cuts(half):
        cut = slice(start, start + part)
        arrived.append((hop([f[:, cut] for f in flight[0]]), n // 2, (0, 1), start))
        start = start + part

    own_other = swap(halves)
    left_own = turn_call(halves, wide)
    left_other = turn_call(own_other, wide)

    common = (wide, left_own, left_other, prior, rows, 512)
    unit = half // LANES
    columns = (2 * me + jnp.arange(2, dtype=jnp.int32)) * unit
    out = tile_call(None, columns, coef, halves, own_other, *common)
    for pair, step, sides, start in arrived:
        block = owner(jnp.array([step, -step], jnp.int32))
        columns = (2 * block + jnp.array(sides, jnp.int32)) * unit + start // LANES
        other = swap(pair)
        out = tile_call(out, columns, coef, pair, other, *common)
    return out


def solution(mesh):
    n, slabs = mesh.shape["assets"], mesh.shape["tm"]

    def rings(width):
        return slabs == 2 and n % 2 == 0 and 4 <= n <= 16 and width % (8 * LANES) == 0

    def local(returns, prior):
        if not rings(returns.shape[1]):
            return local_any(returns, prior)
        return local_ring(returns, prior)

    placed = (P("tm", ("groups", "assets")), P(("groups", "assets"), None))
    return jax.shard_map(
        local,
        mesh=mesh,
        in_specs=placed,
        out_specs=P("tm", ("groups", "assets"), None),
        check_vma=False,
    )
```

```python
import functools

import jax
import jax.numpy as jnp
from jax import lax
from jax.experimental import pallas as pl
from jax.experimental.pallas import tpu as pltpu
from jax.sharding import PartitionSpec as P


LANES = 128
GRANT = 34 * 2**20
LAST_HOPS = 2


def weights(minutes):
    lam = jnp.float32(0.9995)
    position = jnp.arange(minutes, dtype=jnp.float32)
    weight = jnp.sqrt(
        (jnp.float32(1.0) - lam) * jnp.power(lam, jnp.float32(minutes - 1) - position)
    )
    return weight, jnp.power(lam, jnp.float32(minutes))


def scale(part, weight):
    return (part.astype(jnp.float32) * weight[:, None]).astype(jnp.bfloat16)


def prefix(shard, axis, combine, identity):
    length, mine = (lax.axis_size(axis), lax.axis_index(axis))
    everything = jax.tree.map(
        lambda part: lax.all_gather(part.astype(jnp.bfloat16), axis), shard
    )
    start = jax.tree.map(
        lambda part, zero: jnp.broadcast_to(jnp.asarray(zero, part.dtype), part.shape),
        shard,
        identity,
    )

    def turn(k, before):
        reached = k < mine
        new = combine(
            before, jax.tree.map(lambda part, own: part[k].astype(own.dtype), everything, shard)
        )
        return jax.tree.map(lambda a, b: jnp.where(reached, a, b), new, before)

    return lax.fori_loop(0, length, turn, start)


def combine_carry(earlier, later):
    return (later[1] * earlier[0] + later[0], earlier[1] * later[1])


def local_any(returns, prior):
    weight, factor = weights(returns.shape[0])
    scaled = scale(returns, weight)
    tile = lax.dot_general(
        scaled,
        lax.all_gather(scaled, "assets", axis=1, tiled=True),
        (((0,), (0,)), ((), ())),
        preferred_element_type=jnp.float32,
    )
    decay = jnp.full((1,), factor, jnp.float32)
    identity = (jnp.zeros_like(tile), jnp.ones((1,), jnp.float32))
    before, reach = prefix((tile, decay), "tm", combine_carry, identity)
    return (factor * (before + reach[0] * prior) + tile)[None]


def split_kernel(returns, weight, *refs):
    parts, (box, sem) = refs[:-2], refs[-2:]
    width = parts[0].shape[1]
    copies = []
    for k in range(len(parts)):
        at = slice(k * width, (k + 1) * width)
        copies.append(pltpu.make_async_copy(returns.at[:, at], box.at[:, at], sem.at[k]))
        copies[-1].start()
    for k, part in enumerate(parts):
        copies[k].wait()
        for lane in range(0, width, LANES):
            source = box[:, k * width + lane : k * width + lane + LANES]
            part[:, lane : lane + LANES] = (
                source.astype(jnp.float32) * weight[...]
            ).astype(jnp.bfloat16)


def split_call(returns, weight, count):
    minutes, width = returns.shape
    near = pl.BlockSpec(memory_space=pltpu.VMEM)
    part = jax.ShapeDtypeStruct((minutes, width // count), jnp.bfloat16)
    return pl.pallas_call(
        split_kernel,
        out_shape=[part] * count,
        in_specs=[pl.BlockSpec(memory_space=pltpu.HBM), near],
        out_specs=[near] * count,
        scratch_shapes=[
            pltpu.VMEM((minutes, width), jnp.bfloat16),
            pltpu.SemaphoreType.DMA((count,)),
        ],
        compiler_params=pltpu.CompilerParams(vmem_limit_bytes=GRANT),
        cost_estimate=pl.CostEstimate(
            flops=minutes * width, bytes_accessed=4 * minutes * width, transcendentals=0
        ),
    )(returns, weight)


def turn_kernel(*refs):
    parts, out = refs[:-1], refs[-1]
    width = parts[0].shape[1]
    for k, part in enumerate(parts):
        for lane in range(0, width, LANES):
            at = slice(k * width + lane, k * width + lane + LANES)
            out[at, :] = part[:, lane : lane + LANES].T


def turn_call(parts):
    minutes, width = parts[0].shape
    near = pl.BlockSpec(memory_space=pltpu.VMEM)
    return pl.pallas_call(
        turn_kernel,
        out_shape=jax.ShapeDtypeStruct((len(parts) * width, minutes), jnp.bfloat16),
        in_specs=[near] * len(parts),
        out_specs=near,
        compiler_params=pltpu.CompilerParams(vmem_limit_bytes=GRANT),
        cost_estimate=pl.CostEstimate(
            flops=len(parts) * minutes * width,
            bytes_accessed=4 * len(parts) * minutes * width,
            transcendentals=0,
        ),
    )(*parts)


def tile_kernel(count, rows, columns, coef, *refs):
    own, other = refs[:count], refs[count : 2 * count]
    left_own, left_other, prior = refs[2 * count : 2 * count + 3]
    out, box, in_sem, out_sem = refs[-4:]
    width = own[0].shape[1]
    tiles = prior.shape[0] // rows
    earlier = coef[1] != 0.0
    copy = pltpu.make_async_copy

    def place(k):
        return pl.ds(pl.multiple_of(columns[k] * LANES, LANES), width)

    def fetch(k, i):
        at = pl.ds(i * rows, rows)
        return copy(prior.at[at, place(k)], box.at[k, at], in_sem.at[k, i])

    def flush(k, i):
        at = pl.ds(i * rows, rows)
        return copy(box.at[k, at], out.at[0, at, place(k)], out_sem.at[k, i])

    for k in range(count):
        for i in range(tiles):
            fetch(k, i).start()

    for k in range(count):

        @pl.loop(0, tiles)
        def _(i):
            at = pl.ds(pl.multiple_of(i * rows, rows), rows)
            fetch(k, i).wait()

            @pl.when(earlier)
            def _():
                box[k, at] = (
                    coef[0] * box[k, at]
                    + jnp.dot(left_own[at], own[k][...], preferred_element_type=jnp.float32)
                    + coef[1]
                    * jnp.dot(left_other[at], other[k][...], preferred_element_type=jnp.float32)
                )

            @pl.when(jnp.logical_not(earlier))
            def _():
                box[k, at] = coef[0] * box[k, at] + jnp.dot(
                    left_own[at], own[k][...], preferred_element_type=jnp.float32
                )

            flush(k, i).start()

    for k in range(count):
        for i in range(tiles):
            flush(k, i).wait()


def tile_call(out, columns, coef, own, other, left_own, left_other, prior, rows):
    count = len(own)
    minutes, width = own[0].shape
    height, total = prior.shape
    near = pl.BlockSpec(memory_space=pltpu.VMEM)
    far = pl.BlockSpec(memory_space=pltpu.HBM)
    scalar = pl.BlockSpec(memory_space=pltpu.SMEM)
    args = [columns, coef, *own, *other, left_own, left_other, prior]
    in_specs = [scalar] * 2 + [near] * (2 * count + 2) + [far]
    aliases = {}
    if out is not None:
        aliases = {len(args): 0}
        in_specs.append(far)
        args.append(out)
    return pl.pallas_call(
        functools.partial(tile_kernel, count, rows),
        out_shape=jax.ShapeDtypeStruct((1, height, total), jnp.float32),
        in_specs=in_specs,
        out_specs=far,
        scratch_shapes=[
            pltpu.VMEM((count, height, width), jnp.float32),
            pltpu.SemaphoreType.DMA((count, height // rows)),
            pltpu.SemaphoreType.DMA((count, height // rows)),
        ],
        input_output_aliases=aliases,
        compiler_params=pltpu.CompilerParams(vmem_limit_bytes=GRANT),
        cost_estimate=pl.CostEstimate(
            flops=4 * count * minutes * width * height,
            bytes_accessed=count * (8 * width * height + 4 * width * minutes),
            transcendentals=0,
        ),
    )(*args)


def last_cuts(half):
    return (half // LAST_HOPS,) * LAST_HOPS


def local_ring(returns, prior):
    minutes, width = returns.shape
    n = lax.axis_size("assets")
    me, slab = lax.axis_index("assets"), lax.axis_index("tm")
    half = width // 2
    rows = min(prior.shape[0], 512)

    cycle = list(range(0, n, 2)) + list(range(n - 1, 0, -2))
    forward = [(cycle[k], cycle[(k + 1) % n]) for k in range(n)]
    backward = [(b, a) for a, b in forward]
    place = jnp.where(me % 2 == 0, me // 2, n - 1 - me // 2)

    def owner(step):
        at = lax.rem(place - step + 2 * n, n)
        return jnp.where(at < n // 2, 2 * at, 2 * (n - 1 - at) + 1)

    def swap(pieces):
        moved = []
        for part in pieces:
            moved.append(lax.ppermute(part, "tm", [(0, 1), (1, 0)]))
        return moved

    weight, factor = weights(minutes)
    wide = jnp.broadcast_to(weight[:, None], (minutes, LANES))
    coef = jnp.where(slab == 0, jnp.stack([factor, 0.0]), jnp.stack([factor * factor, factor]))

    def hop(parts):
        moved = []
        for way, pairs in enumerate((forward, backward)):
            moved.append(lax.ppermute(parts[way], "assets", pairs))
        return moved

    halves = split_call(returns, wide, 2)
    flight = [halves, halves[::-1]]
    arrived = []
    for k in range(n - 2):
        flight[k % 2] = hop(flight[k % 2])
        arrived.append((flight[k % 2], k // 2 + 1, (k % 2, 1 - k % 2), 0))
    start = 0
    for part in last_cuts(half):
        cut = slice(start, start + part)
        arrived.append((hop([f[:, cut] for f in flight[0]]), n // 2, (0, 1), start))
        start = start + part

    own_other = swap(halves)
    left_own = turn_call(halves)
    left_other = turn_call(own_other)

    common = (left_own, left_other, prior, rows)
    unit = half // LANES
    columns = (2 * me + jnp.arange(2, dtype=jnp.int32)) * unit
    out = tile_call(None, columns, coef, halves, own_other, *common)
    for pair, step, sides, start in arrived:
        block = owner(jnp.array([step, -step], jnp.int32))
        columns = (2 * block + jnp.array(sides, jnp.int32)) * unit + start // LANES
        other = swap(pair)
        out = tile_call(out, columns, coef, pair, other, *common)
    return out


def solution(mesh):
    n, slabs = mesh.shape["assets"], mesh.shape["tm"]

    def rings(width):
        return slabs == 2 and n % 2 == 0 and 4 <= n <= 16 and width % (8 * LANES) == 0

    def local(returns, prior):
        if not rings(returns.shape[1]):
            return local_any(returns, prior)
        return local_ring(returns, prior)

    placed = (P("tm", ("groups", "assets")), P(("groups", "assets"), None))
    return jax.shard_map(
        local,
        mesh=mesh,
        in_specs=placed,
        out_specs=P("tm", ("groups", "assets"), None),
        check_vma=False,
    )
```

```python
import functools

import jax
import jax.numpy as jnp
from jax import lax
from jax.experimental import pallas as pl
from jax.experimental.pallas import tpu as pltpu
from jax.sharding import PartitionSpec as P


LANES = 128
GRANT = 34 * 2**20
SPLIT_GRANT = 123 * 2**19
LAST_HOPS = 2


def weights(minutes):
    lam = jnp.float32(0.9995)
    position = jnp.arange(minutes, dtype=jnp.float32)
    weight = jnp.sqrt(
        (jnp.float32(1.0) - lam) * jnp.power(lam, jnp.float32(minutes - 1) - position)
    )
    return weight, jnp.power(lam, jnp.float32(minutes))


def scale(part, weight):
    return (part.astype(jnp.float32) * weight[:, None]).astype(jnp.bfloat16)


def prefix(shard, axis, combine, identity):
    length, mine = (lax.axis_size(axis), lax.axis_index(axis))
    everything = jax.tree.map(
        lambda part: lax.all_gather(part.astype(jnp.bfloat16), axis), shard
    )
    start = jax.tree.map(
        lambda part, zero: jnp.broadcast_to(jnp.asarray(zero, part.dtype), part.shape),
        shard,
        identity,
    )

    def turn(k, before):
        reached = k < mine
        new = combine(
            before, jax.tree.map(lambda part, own: part[k].astype(own.dtype), everything, shard)
        )
        return jax.tree.map(lambda a, b: jnp.where(reached, a, b), new, before)

    return lax.fori_loop(0, length, turn, start)


def combine_carry(earlier, later):
    return (later[1] * earlier[0] + later[0], earlier[1] * later[1])


def local_any(returns, prior):
    weight, factor = weights(returns.shape[0])
    scaled = scale(returns, weight)
    tile = lax.dot_general(
        scaled,
        lax.all_gather(scaled, "assets", axis=1, tiled=True),
        (((0,), (0,)), ((), ())),
        preferred_element_type=jnp.float32,
    )
    decay = jnp.full((1,), factor, jnp.float32)
    identity = (jnp.zeros_like(tile), jnp.ones((1,), jnp.float32))
    before, reach = prefix((tile, decay), "tm", combine_carry, identity)
    return (factor * (before + reach[0] * prior) + tile)[None]


def split_kernel(returns, weight, *refs):
    parts, (box, sem) = refs[:-2], refs[-2:]
    width = parts[0].shape[1]
    copies = []
    for k in range(sem.shape[0]):
        at = slice(k * 2 * LANES, (k + 1) * 2 * LANES)
        copies.append(pltpu.make_async_copy(returns.at[:, at], box.at[:, at], sem.at[k]))
        copies[-1].start()
    for k, copy in enumerate(copies):
        copy.wait()
        for lane in range(k * 2 * LANES, (k + 1) * 2 * LANES, LANES):
            part, start = parts[lane // width], lane % width
            part[:, start : start + LANES] = (
                box[:, lane : lane + LANES].astype(jnp.float32) * weight[...]
            ).astype(jnp.bfloat16)


def split_call(returns, weight, count):
    minutes, width = returns.shape
    near = pl.BlockSpec(memory_space=pltpu.VMEM)
    part = jax.ShapeDtypeStruct((minutes, width // count), jnp.bfloat16)
    return pl.pallas_call(
        split_kernel,
        out_shape=[part] * count,
        in_specs=[pl.BlockSpec(memory_space=pltpu.HBM), near],
        out_specs=[near] * count,
        scratch_shapes=[
            pltpu.VMEM((minutes, width), jnp.bfloat16),
            pltpu.SemaphoreType.DMA((width // (2 * LANES),)),
        ],
        compiler_params=pltpu.CompilerParams(vmem_limit_bytes=SPLIT_GRANT),
        cost_estimate=pl.CostEstimate(
            flops=minutes * width, bytes_accessed=4 * minutes * width, transcendentals=0
        ),
    )(returns, weight)


def turn_kernel(*refs):
    parts, out = refs[:-1], refs[-1]
    width = parts[0].shape[1]
    for k, part in enumerate(parts):
        for lane in range(0, width, LANES):
            at = slice(k * width + lane, k * width + lane + LANES)
            out[at, :] = part[:, lane : lane + LANES].T


def turn_call(parts):
    minutes, width = parts[0].shape
    near = pl.BlockSpec(memory_space=pltpu.VMEM)
    return pl.pallas_call(
        turn_kernel,
        out_shape=jax.ShapeDtypeStruct((len(parts) * width, minutes), jnp.bfloat16),
        in_specs=[near] * len(parts),
        out_specs=near,
        compiler_params=pltpu.CompilerParams(vmem_limit_bytes=GRANT),
        cost_estimate=pl.CostEstimate(
            flops=len(parts) * minutes * width,
            bytes_accessed=4 * len(parts) * minutes * width,
            transcendentals=0,
        ),
    )(*parts)


def tile_kernel(count, rows, columns, coef, *refs):
    own, other = refs[:count], refs[count : 2 * count]
    left_own, left_other, prior = refs[2 * count : 2 * count + 3]
    out, box, in_sem, out_sem = refs[-4:]
    width = own[0].shape[1]
    tiles = prior.shape[0] // rows
    earlier = coef[1] != 0.0
    copy = pltpu.make_async_copy

    def place(k):
        return pl.ds(pl.multiple_of(columns[k] * LANES, LANES), width)

    def fetch(k, i):
        at = pl.ds(i * rows, rows)
        return copy(prior.at[at, place(k)], box.at[k, at], in_sem.at[k, i])

    def flush(k, i):
        at = pl.ds(i * rows, rows)
        return copy(box.at[k, at], out.at[0, at, place(k)], out_sem.at[k, i])

    for k in range(count):
        for i in range(tiles):
            fetch(k, i).start()

    for k in range(count):

        @pl.loop(0, tiles)
        def _(i):
            at = pl.ds(pl.multiple_of(i * rows, rows), rows)
            first = jnp.dot(left_own[at], own[k][...], preferred_element_type=jnp.float32)

            @pl.when(earlier)
            def _():
                both = first + coef[1] * jnp.dot(
                    left_other[at], other[k][...], preferred_element_type=jnp.float32
                )
                fetch(k, i).wait()
                box[k, at] = coef[0] * box[k, at] + both

            @pl.when(jnp.logical_not(earlier))
            def _():
                fetch(k, i).wait()
                box[k, at] = coef[0] * box[k, at] + first

            flush(k, i).start()

    for k in range(count):
        for i in range(tiles):
            flush(k, i).wait()


def tile_call(out, columns, coef, own, other, left_own, left_other, prior, rows):
    count = len(own)
    minutes, width = own[0].shape
    height, total = prior.shape
    near = pl.BlockSpec(memory_space=pltpu.VMEM)
    far = pl.BlockSpec(memory_space=pltpu.HBM)
    scalar = pl.BlockSpec(memory_space=pltpu.SMEM)
    args = [columns, coef, *own, *other, left_own, left_other, prior]
    in_specs = [scalar] * 2 + [near] * (2 * count + 2) + [far]
    aliases = {}
    if out is not None:
        aliases = {len(args): 0}
        in_specs.append(far)
        args.append(out)
    return pl.pallas_call(
        functools.partial(tile_kernel, count, rows),
        out_shape=jax.ShapeDtypeStruct((1, height, total), jnp.float32),
        in_specs=in_specs,
        out_specs=far,
        scratch_shapes=[
            pltpu.VMEM((count, height, width), jnp.float32),
            pltpu.SemaphoreType.DMA((count, height // rows)),
            pltpu.SemaphoreType.DMA((count, height // rows)),
        ],
        input_output_aliases=aliases,
        compiler_params=pltpu.CompilerParams(vmem_limit_bytes=GRANT),
        cost_estimate=pl.CostEstimate(
            flops=4 * count * minutes * width * height,
            bytes_accessed=count * (8 * width * height + 4 * width * minutes),
            transcendentals=0,
        ),
    )(*args)


def decayed_kernel(columns, coef, prior, out, sem):
    count, _, width = out.shape

    def fetch(k):
        at = pl.ds(pl.multiple_of(columns[k] * LANES, LANES), width)
        return pltpu.make_async_copy(prior.at[:, at], out.at[k], sem.at[k])

    for k in range(count):
        fetch(k).start()
    for k in range(count):
        fetch(k).wait()
        out[k] = coef[0] * out[k]


def own_kernel(count, *refs):
    own, left, base, out = refs[:count], *refs[count:]
    for k in range(count):
        out[k] = base[k] + jnp.dot(left[...], own[k][...], preferred_element_type=jnp.float32)


def other_kernel(count, rows, columns, coef, *refs):
    other, left, base = refs[:count], *refs[count : count + 2]
    out, box, sem = refs[-3:]
    height, width = box.shape[1:]
    earlier = coef[1] != 0.0

    def flush(source, k, i):
        at = pl.ds(i * rows, rows)
        across = pl.ds(pl.multiple_of(columns[k] * LANES, LANES), width)
        return pltpu.make_async_copy(source.at[k, at], out.at[0, at, across], sem.at[k, i])

    for k in range(count):

        @pl.loop(0, height // rows)
        def _(i):
            at = pl.ds(pl.multiple_of(i * rows, rows), rows)

            @pl.when(earlier)
            def _():
                box[k, at] = base[k, at] + coef[1] * jnp.dot(
                    left[at], other[k][...], preferred_element_type=jnp.float32
                )
                flush(box, k, i).start()

            @pl.when(jnp.logical_not(earlier))
            def _():
                flush(base, k, i).start()

    for k in range(count):
        for i in range(height // rows):
            flush(box, k, i).wait()


def last_calls(columns, coef, own, left_own, left_other, prior, rows):
    count = len(own)
    minutes, width = own[0].shape
    height, _ = prior.shape
    near = pl.BlockSpec(memory_space=pltpu.VMEM)
    far = pl.BlockSpec(memory_space=pltpu.HBM)
    scalar = pl.BlockSpec(memory_space=pltpu.SMEM)
    small = jax.ShapeDtypeStruct((count, height, width), jnp.float32)
    grant = pltpu.CompilerParams(vmem_limit_bytes=GRANT)
    size = 4 * count * height * width

    def cost(flops, bytes_accessed):
        return pl.CostEstimate(flops=flops, bytes_accessed=bytes_accessed, transcendentals=0)

    base = pl.pallas_call(
        decayed_kernel,
        out_shape=small,
        in_specs=[scalar, scalar, far],
        out_specs=near,
        scratch_shapes=[pltpu.SemaphoreType.DMA((count,))],
        compiler_params=grant,
        cost_estimate=cost(size // 4, size),
    )(columns, coef, prior)
    flops = 2 * count * minutes * width * height
    base = pl.pallas_call(
        functools.partial(own_kernel, count),
        out_shape=small,
        in_specs=[near] * (count + 2),
        out_specs=near,
        compiler_params=grant,
        cost_estimate=cost(flops, 2 * size),
    )(*own, left_own, base)

    def finish(out, other):
        args = [columns, coef, *other, left_other, base, out]
        return pl.pallas_call(
            functools.partial(other_kernel, count, rows),
            out_shape=jax.ShapeDtypeStruct(out.shape, out.dtype),
            in_specs=[scalar, scalar] + [near] * (count + 2) + [far],
            out_specs=far,
            scratch_shapes=[
                pltpu.VMEM(small.shape, small.dtype),
                pltpu.SemaphoreType.DMA((count, height // rows)),
            ],
            input_output_aliases={len(args) - 1: 0},
            compiler_params=grant,
            cost_estimate=cost(flops, 2 * size),
        )(*args)

    return finish


def last_cuts(half):
    return (half // LAST_HOPS,) * LAST_HOPS


def local_ring(returns, prior):
    minutes, width = returns.shape
    n = lax.axis_size("assets")
    me, slab = lax.axis_index("assets"), lax.axis_index("tm")
    half = width // 2
    rows = min(prior.shape[0], 512)

    cycle = list(range(0, n, 2)) + list(range(n - 1, 0, -2))
    forward = [(cycle[k], cycle[(k + 1) % n]) for k in range(n)]
    backward = [(b, a) for a, b in forward]
    place = jnp.where(me % 2 == 0, me // 2, n - 1 - me // 2)

    def owner(step):
        at = lax.rem(place - step + 2 * n, n)
        return jnp.where(at < n // 2, 2 * at, 2 * (n - 1 - at) + 1)

    def swap(pieces):
        moved = []
        for part in pieces:
            moved.append(lax.ppermute(part, "tm", [(0, 1), (1, 0)]))
        return moved

    weight, factor = weights(minutes)
    wide = jnp.broadcast_to(weight[:, None], (minutes, LANES))
    coef = jnp.where(slab == 0, jnp.stack([factor, 0.0]), jnp.stack([factor * factor, factor]))

    def hop(parts):
        moved = []
        for way, pairs in enumerate((forward, backward)):
            moved.append(lax.ppermute(parts[way], "assets", pairs))
        return moved

    halves = split_call(returns, wide, 2)
    flight = [halves, halves[::-1]]
    arrived = []
    for k in range(n - 2):
        flight[k % 2] = hop(flight[k % 2])
        arrived.append((flight[k % 2], k // 2 + 1, (k % 2, 1 - k % 2), 0))
    start = 0
    for part in last_cuts(half):
        cut = slice(start, start + part)
        arrived.append((hop([f[:, cut] for f in flight[0]]), n // 2, (0, 1), start))
        start = start + part

    own_other = swap(halves)
    left_own = turn_call(halves)
    left_other = turn_call(own_other)

    common = (left_own, left_other, prior, rows)
    unit = half // LANES
    columns = (2 * me + jnp.arange(2, dtype=jnp.int32)) * unit
    out = tile_call(None, columns, coef, halves, own_other, *common)
    for k, (pair, step, sides, start) in enumerate(arrived):
        block = owner(jnp.array([step, -step], jnp.int32))
        columns = (2 * block + jnp.array(sides, jnp.int32)) * unit + start // LANES
        if k == len(arrived) - 1:
            finish = last_calls(columns, coef, pair, *common)
            return finish(out, swap(pair))
        other = swap(pair)
        out = tile_call(out, columns, coef, pair, other, *common)


def solution(mesh):
    n, slabs = mesh.shape["assets"], mesh.shape["tm"]

    def rings(width):
        return slabs == 2 and n % 2 == 0 and 4 <= n <= 16 and width % (8 * LANES) == 0

    def local(returns, prior):
        if not rings(returns.shape[1]):
            return local_any(returns, prior)
        return local_ring(returns, prior)

    placed = (P("tm", ("groups", "assets")), P(("groups", "assets"), None))
    return jax.shard_map(
        local,
        mesh=mesh,
        in_specs=placed,
        out_specs=P("tm", ("groups", "assets"), None),
        check_vma=False,
    )
```

```python
import functools

import jax
import jax.numpy as jnp
import numpy as np
from jax import lax
from jax.experimental import pallas as pl
from jax.experimental.pallas import tpu as pltpu
from jax.sharding import PartitionSpec as P


LANES = 128
GRANT = 16 * 2**20
LAST_HOPS = 2


def weights(minutes):
    lam = jnp.float32(0.9995)
    position = jnp.arange(minutes, dtype=jnp.float32)
    weight = jnp.sqrt(
        (jnp.float32(1.0) - lam) * jnp.power(lam, jnp.float32(minutes - 1) - position)
    )
    return weight, jnp.power(lam, jnp.float32(minutes))


def constants(minutes):
    lam = np.float32(0.9995)
    position = np.arange(minutes, dtype=np.float32)
    weight = np.sqrt(
        (np.float32(1.0) - lam) * np.power(lam, np.float32(minutes - 1) - position)
    )
    return weight.astype(np.float32), np.power(lam, np.float32(minutes))


def scale(part, weight):
    return (part.astype(jnp.float32) * weight[:, None]).astype(jnp.bfloat16)


def prefix(shard, axis, combine, identity):
    length, mine = (lax.axis_size(axis), lax.axis_index(axis))
    everything = jax.tree.map(
        lambda part: lax.all_gather(part.astype(jnp.bfloat16), axis), shard
    )
    start = jax.tree.map(
        lambda part, zero: jnp.broadcast_to(jnp.asarray(zero, part.dtype), part.shape),
        shard,
        identity,
    )

    def turn(k, before):
        reached = k < mine
        new = combine(
            before, jax.tree.map(lambda part, own: part[k].astype(own.dtype), everything, shard)
        )
        return jax.tree.map(lambda a, b: jnp.where(reached, a, b), new, before)

    return lax.fori_loop(0, length, turn, start)


def combine_carry(earlier, later):
    return (later[1] * earlier[0] + later[0], earlier[1] * later[1])


def local_any(returns, prior):
    weight, factor = weights(returns.shape[0])
    scaled = scale(returns, weight)
    tile = lax.dot_general(
        scaled,
        lax.all_gather(scaled, "assets", axis=1, tiled=True),
        (((0,), (0,)), ((), ())),
        preferred_element_type=jnp.float32,
    )
    decay = jnp.full((1,), factor, jnp.float32)
    identity = (jnp.zeros_like(tile), jnp.ones((1,), jnp.float32))
    before, reach = prefix((tile, decay), "tm", combine_carry, identity)
    return (factor * (before + reach[0] * prior) + tile)[None]


def owner(step):
    n, me = lax.axis_size("assets"), lax.axis_index("assets")
    place = jnp.where(me % 2 == 0, me // 2, n - 1 - me // 2)
    at = lax.rem(place - step + 2 * n, n)
    return jnp.where(at < n // 2, 2 * at, 2 * (n - 1 - at) + 1)


def columns_of(where, k, width):
    step, block, offset = where[k]
    return pl.ds(pl.multiple_of(owner(step) * block + offset, LANES), width)


def decay(factor):
    first = lax.axis_index("tm") == 0
    return jnp.where(first, factor, factor * factor), jnp.logical_not(first)


def in_hbm(x):
    return pltpu.with_memory_space_constraint(x, pltpu.HBM)


def split_kernel(returns, weight, *refs):
    parts, (box, wide, sem) = refs[:-3], refs[-3:]
    width = parts[0].shape[1]
    copies = []
    for k in range(sem.shape[0]):
        at = slice(k * 2 * LANES, (k + 1) * 2 * LANES)
        copies.append(pltpu.make_async_copy(returns.at[:, at], box.at[:, at], sem.at[k]))
        copies[-1].start()
    for k in range(weight.shape[0]):
        wide[k * LANES : (k + 1) * LANES, :] = jnp.broadcast_to(
            weight[k : k + 1, :], (LANES, LANES)
        ).T
    for k, copy in enumerate(copies):
        copy.wait()
        for lane in range(k * 2 * LANES, (k + 1) * 2 * LANES, LANES):
            part, start = parts[lane // width], lane % width
            part[:, start : start + LANES] = (
                box[:, lane : lane + LANES].astype(jnp.float32) * wide[...]
            ).astype(jnp.bfloat16)


def split_call(returns, weight, count):
    minutes, width = returns.shape
    near = pl.BlockSpec(memory_space=pltpu.VMEM)
    part = pltpu.VMEM((minutes, width // count), jnp.bfloat16)
    return pl.pallas_call(
        split_kernel,
        out_shape=[part] * count,
        in_specs=[pl.BlockSpec(memory_space=pltpu.HBM), near],
        out_specs=[near] * count,
        scratch_shapes=[
            pltpu.VMEM((minutes, width), jnp.bfloat16),
            pltpu.VMEM((minutes, LANES), jnp.float32),
            pltpu.SemaphoreType.DMA((width // (2 * LANES),)),
        ],
        compiler_params=pltpu.CompilerParams(vmem_limit_bytes=GRANT),
        cost_estimate=pl.CostEstimate(
            flops=minutes * width, bytes_accessed=4 * minutes * width, transcendentals=0
        ),
    )(in_hbm(returns), weight)


def turn_kernel(*refs):
    parts, out = refs[:-1], refs[-1]
    width = parts[0].shape[1]
    for k, part in enumerate(parts):
        for lane in range(0, width, LANES):
            at = slice(k * width + lane, k * width + lane + LANES)
            out[at, :] = part[:, lane : lane + LANES].T


def turn_call(parts):
    minutes, width = parts[0].shape
    near = pl.BlockSpec(memory_space=pltpu.VMEM)
    return pl.pallas_call(
        turn_kernel,
        out_shape=pltpu.VMEM((len(parts) * width, minutes), jnp.bfloat16),
        in_specs=[near] * len(parts),
        out_specs=near,
        compiler_params=pltpu.CompilerParams(vmem_limit_bytes=GRANT),
        cost_estimate=pl.CostEstimate(
            flops=len(parts) * minutes * width,
            bytes_accessed=4 * len(parts) * minutes * width,
            transcendentals=0,
        ),
    )(*parts)


def tile_kernel(where, rows, factor, *refs):
    count = len(where)
    own, other = refs[:count], refs[count : 2 * count]
    left_own, left_other, prior = refs[2 * count : 2 * count + 3]
    out, box, in_sem, out_sem = refs[-4:]
    width = own[0].shape[1]
    tiles = prior.shape[0] // rows
    kept, earlier = decay(factor)
    copy = pltpu.make_async_copy

    def place(k):
        return columns_of(where, k, width)

    def fetch(k, i):
        at = pl.ds(i * rows, rows)
        return copy(prior.at[at, place(k)], box.at[k, at], in_sem.at[k, i])

    def flush(k, i):
        at = pl.ds(i * rows, rows)
        return copy(box.at[k, at], out.at[0, at, place(k)], out_sem.at[k, i])

    for k in range(count):
        for i in range(tiles):
            fetch(k, i).start()

    for k in range(count):

        @pl.loop(0, tiles)
        def _(i):
            at = pl.ds(pl.multiple_of(i * rows, rows), rows)
            first = jnp.dot(left_own[at], own[k][...], preferred_element_type=jnp.float32)

            @pl.when(earlier)
            def _():
                both = first + factor * jnp.dot(
                    left_other[at], other[k][...], preferred_element_type=jnp.float32
                )
                fetch(k, i).wait()
                box[k, at] = kept * box[k, at] + both

            @pl.when(jnp.logical_not(earlier))
            def _():
                fetch(k, i).wait()
                box[k, at] = kept * box[k, at] + first

            flush(k, i).start()

    for k in range(count):
        for i in range(tiles):
            flush(k, i).wait()


def tile_call(out, where, own, other, left_own, left_other, prior, rows, factor):
    count = len(own)
    minutes, width = own[0].shape
    height, total = prior.shape
    near = pl.BlockSpec(memory_space=pltpu.VMEM)
    far = pl.BlockSpec(memory_space=pltpu.HBM)
    args = [*own, *other, left_own, left_other, prior]
    in_specs = [near] * (2 * count + 2) + [far]
    aliases = {}
    if out is not None:
        aliases = {len(args): 0}
        in_specs.append(far)
        args.append(out)
    return pl.pallas_call(
        functools.partial(tile_kernel, where, rows, factor),
        out_shape=pltpu.HBM((1, height, total), jnp.float32),
        in_specs=in_specs,
        out_specs=far,
        scratch_shapes=[
            pltpu.VMEM((count, height, width), jnp.float32),
            pltpu.SemaphoreType.DMA((count, height // rows)),
            pltpu.SemaphoreType.DMA((count, height // rows)),
        ],
        input_output_aliases=aliases,
        compiler_params=pltpu.CompilerParams(vmem_limit_bytes=GRANT),
        cost_estimate=pl.CostEstimate(
            flops=4 * count * minutes * width * height,
            bytes_accessed=count * (8 * width * height + 4 * width * minutes),
            transcendentals=0,
        ),
    )(*args)


def decayed_kernel(where, factor, prior, out, sem):
    count, _, width = out.shape
    kept, _ = decay(factor)

    def fetch(k):
        at = columns_of(where, k, width)
        return pltpu.make_async_copy(prior.at[:, at], out.at[k], sem.at[k])

    for k in range(count):
        fetch(k).start()
    for k in range(count):
        fetch(k).wait()
        out[k] = kept * out[k]


def own_kernel(count, *refs):
    own, left, base, out = refs[:count], *refs[count:]
    for k in range(count):
        out[k] = base[k] + jnp.dot(left[...], own[k][...], preferred_element_type=jnp.float32)


def other_kernel(where, rows, factor, *refs):
    count = len(where)
    other, left, base = refs[:count], *refs[count : count + 2]
    out, box, sem = refs[-3:]
    height, width = box.shape[1:]
    _, earlier = decay(factor)

    def flush(source, k, i):
        at = pl.ds(i * rows, rows)
        across = columns_of(where, k, width)
        return pltpu.make_async_copy(source.at[k, at], out.at[0, at, across], sem.at[k, i])

    for k in range(count):

        @pl.loop(0, height // rows)
        def _(i):
            at = pl.ds(pl.multiple_of(i * rows, rows), rows)

            @pl.when(earlier)
            def _():
                box[k, at] = base[k, at] + factor * jnp.dot(
                    left[at], other[k][...], preferred_element_type=jnp.float32
                )
                flush(box, k, i).start()

            @pl.when(jnp.logical_not(earlier))
            def _():
                flush(base, k, i).start()

    for k in range(count):
        for i in range(height // rows):
            flush(box, k, i).wait()


def last_calls(where, own, left_own, left_other, prior, rows, factor):
    count = len(own)
    minutes, width = own[0].shape
    height, _ = prior.shape
    near = pl.BlockSpec(memory_space=pltpu.VMEM)
    far = pl.BlockSpec(memory_space=pltpu.HBM)
    small = pltpu.VMEM((count, height, width), jnp.float32)
    grant = pltpu.CompilerParams(vmem_limit_bytes=GRANT)
    size = 4 * count * height * width

    def cost(flops, bytes_accessed):
        return pl.CostEstimate(flops=flops, bytes_accessed=bytes_accessed, transcendentals=0)

    base = pl.pallas_call(
        functools.partial(decayed_kernel, where, factor),
        out_shape=small,
        in_specs=[far],
        out_specs=near,
        scratch_shapes=[pltpu.SemaphoreType.DMA((count,))],
        compiler_params=grant,
        cost_estimate=cost(size // 4, size),
    )(prior)
    flops = 2 * count * minutes * width * height
    base = pl.pallas_call(
        functools.partial(own_kernel, count),
        out_shape=small,
        in_specs=[near] * (count + 2),
        out_specs=near,
        compiler_params=grant,
        cost_estimate=cost(flops, 2 * size),
    )(*own, left_own, base)

    def finish(out, other):
        args = [*other, left_other, base, out]
        return pl.pallas_call(
            functools.partial(other_kernel, where, rows, factor),
            out_shape=pltpu.HBM(out.shape, out.dtype),
            in_specs=[near] * (count + 2) + [far],
            out_specs=far,
            scratch_shapes=[
                pltpu.VMEM(small.shape, small.dtype),
                pltpu.SemaphoreType.DMA((count, height // rows)),
            ],
            input_output_aliases={len(args) - 1: 0},
            compiler_params=grant,
            cost_estimate=cost(flops, 2 * size),
        )(*args)

    return finish


def last_cuts(half):
    return (half // LAST_HOPS,) * LAST_HOPS


def local_ring(returns, prior):
    minutes, width = returns.shape
    n = lax.axis_size("assets")
    half = width // 2
    rows = min(prior.shape[0], 512)

    cycle = list(range(0, n, 2)) + list(range(n - 1, 0, -2))
    forward = [(cycle[k], cycle[(k + 1) % n]) for k in range(n)]
    backward = [(b, a) for a, b in forward]

    def swap(pieces):
        moved = []
        for part in pieces:
            moved.append(lax.ppermute(part, "tm", [(0, 1), (1, 0)]))
        return moved

    weight, factor = constants(minutes)

    def hop(parts):
        moved = []
        for way, pairs in enumerate((forward, backward)):
            moved.append(lax.ppermute(parts[way], "assets", pairs))
        return moved

    halves = split_call(returns, jnp.asarray(weight.reshape(-1, LANES)), 2)
    flight = [halves, halves[::-1]]
    arrived = []
    for k in range(n - 2):
        flight[k % 2] = hop(flight[k % 2])
        arrived.append((flight[k % 2], k // 2 + 1, (k % 2, 1 - k % 2), 0))
    start = 0
    for part in last_cuts(half):
        cut = slice(start, start + part)
        arrived.append((hop([f[:, cut] for f in flight[0]]), n // 2, (0, 1), start))
        start = start + part

    own_other = swap(halves)
    left_own = turn_call(halves)
    left_other = turn_call(own_other)

    prior = in_hbm(prior)
    common = (left_own, left_other, prior, rows, factor)
    where = tuple((0, width, k * half) for k in (0, 1))
    out = tile_call(None, where, halves, own_other, *common)
    for k, (pair, step, sides, start) in enumerate(arrived):
        where = tuple(
            (way_step, width, side * half + start)
            for way_step, side in zip((step, -step), sides, strict=True)
        )
        if k == len(arrived) - 1:
            finish = last_calls(where, pair, *common)
            return finish(out, swap(pair))
        other = swap(pair)
        out = tile_call(out, where, pair, other, *common)


def solution(mesh):
    n, slabs = mesh.shape["assets"], mesh.shape["tm"]

    def rings(minutes, width):
        even = slabs == 2 and n % 2 == 0 and 4 <= n <= 16
        return even and minutes % LANES == 0 and width % (8 * LANES) == 0

    def local(returns, prior):
        if not rings(*returns.shape):
            return local_any(returns, prior)
        return local_ring(returns, prior)

    placed = (P("tm", ("groups", "assets")), P(("groups", "assets"), None))
    return jax.shard_map(
        local,
        mesh=mesh,
        in_specs=placed,
        out_specs=P("tm", ("groups", "assets"), None),
        check_vma=False,
    )
```

```python
import functools

import jax
import jax.numpy as jnp
import numpy as np
from jax import lax
from jax.experimental import pallas as pl
from jax.experimental.pallas import tpu as pltpu
from jax.sharding import PartitionSpec as P


LANES = 128
GRANT = 16 * 2**20
LAST_HOPS = 3


def weights(minutes):
    lam = jnp.float32(0.9995)
    position = jnp.arange(minutes, dtype=jnp.float32)
    weight = jnp.sqrt(
        (jnp.float32(1.0) - lam) * jnp.power(lam, jnp.float32(minutes - 1) - position)
    )
    return weight, jnp.power(lam, jnp.float32(minutes))


def constants(minutes):
    lam = np.float32(0.9995)
    position = np.arange(minutes, dtype=np.float32)
    weight = np.sqrt(
        (np.float32(1.0) - lam) * np.power(lam, np.float32(minutes - 1) - position)
    )
    return weight.astype(np.float32), np.power(lam, np.float32(minutes))


def scale(part, weight):
    return (part.astype(jnp.float32) * weight[:, None]).astype(jnp.bfloat16)


def prefix(shard, axis, combine, identity):
    length, mine = (lax.axis_size(axis), lax.axis_index(axis))
    everything = jax.tree.map(
        lambda part: lax.all_gather(part.astype(jnp.bfloat16), axis), shard
    )
    start = jax.tree.map(
        lambda part, zero: jnp.broadcast_to(jnp.asarray(zero, part.dtype), part.shape),
        shard,
        identity,
    )

    def turn(k, before):
        reached = k < mine
        new = combine(
            before, jax.tree.map(lambda part, own: part[k].astype(own.dtype), everything, shard)
        )
        return jax.tree.map(lambda a, b: jnp.where(reached, a, b), new, before)

    return lax.fori_loop(0, length, turn, start)


def combine_carry(earlier, later):
    return (later[1] * earlier[0] + later[0], earlier[1] * later[1])


def local_any(returns, prior):
    weight, factor = weights(returns.shape[0])
    scaled = scale(returns, weight)
    tile = lax.dot_general(
        scaled,
        lax.all_gather(scaled, "assets", axis=1, tiled=True),
        (((0,), (0,)), ((), ())),
        preferred_element_type=jnp.float32,
    )
    decay = jnp.full((1,), factor, jnp.float32)
    identity = (jnp.zeros_like(tile), jnp.ones((1,), jnp.float32))
    before, reach = prefix((tile, decay), "tm", combine_carry, identity)
    return (factor * (before + reach[0] * prior) + tile)[None]


def owner(step):
    n, me = lax.axis_size("assets"), lax.axis_index("assets")
    place = jnp.where(me % 2 == 0, me // 2, n - 1 - me // 2)
    at = lax.rem(place - step + 2 * n, n)
    return jnp.where(at < n // 2, 2 * at, 2 * (n - 1 - at) + 1)


def columns_of(where, k, width):
    step, block, offset = where[k]
    return pl.ds(pl.multiple_of(owner(step) * block + offset, LANES), width)


def decay(factor):
    first = lax.axis_index("tm") == 0
    return jnp.where(first, factor, factor * factor), jnp.logical_not(first)


def in_hbm(x):
    return pltpu.with_memory_space_constraint(x, pltpu.HBM)


def split_kernel(returns, weight, *refs):
    parts, (box, row, wide, sem, row_sem) = refs[:-5], refs[-5:]
    width = parts[0].shape[1]
    copies = []
    row_copy = pltpu.make_async_copy(weight, row, row_sem)
    row_copy.start()
    for k in range(sem.shape[0]):
        at = slice(k * 2 * LANES, (k + 1) * 2 * LANES)
        copies.append(pltpu.make_async_copy(returns.at[:, at], box.at[:, at], sem.at[k]))
        copies[-1].start()
    row_copy.wait()
    for k in range(row.shape[0]):
        wide[k * LANES : (k + 1) * LANES, :] = jnp.broadcast_to(
            row[k : k + 1, :], (LANES, LANES)
        ).T
    for k, copy in enumerate(copies):
        copy.wait()
        for lane in range(k * 2 * LANES, (k + 1) * 2 * LANES, LANES):
            part, start = parts[lane // width], lane % width
            part[:, start : start + LANES] = (
                box[:, lane : lane + LANES].astype(jnp.float32) * wide[...]
            ).astype(jnp.bfloat16)


def split_call(returns, weight, count):
    minutes, width = returns.shape
    near = pl.BlockSpec(memory_space=pltpu.VMEM)
    part = pltpu.VMEM((minutes, width // count), jnp.bfloat16)
    return pl.pallas_call(
        split_kernel,
        out_shape=[part] * count,
        in_specs=[pl.BlockSpec(memory_space=pltpu.HBM)] * 2,
        out_specs=[near] * count,
        scratch_shapes=[
            pltpu.VMEM((minutes, width), jnp.bfloat16),
            pltpu.VMEM(weight.shape, weight.dtype),
            pltpu.VMEM((minutes, LANES), jnp.float32),
            pltpu.SemaphoreType.DMA((width // (2 * LANES),)),
            pltpu.SemaphoreType.DMA,
        ],
        compiler_params=pltpu.CompilerParams(vmem_limit_bytes=GRANT),
        cost_estimate=pl.CostEstimate(
            flops=minutes * width, bytes_accessed=4 * minutes * width, transcendentals=0
        ),
    )(in_hbm(returns), in_hbm(weight))


def turn_kernel(*refs):
    parts, out = refs[:-1], refs[-1]
    width = parts[0].shape[1]
    for k, part in enumerate(parts):
        for lane in range(0, width, LANES):
            at = slice(k * width + lane, k * width + lane + LANES)
            out[at, :] = part[:, lane : lane + LANES].T


def turn_call(parts):
    minutes, width = parts[0].shape
    near = pl.BlockSpec(memory_space=pltpu.VMEM)
    return pl.pallas_call(
        turn_kernel,
        out_shape=pltpu.VMEM((len(parts) * width, minutes), jnp.bfloat16),
        in_specs=[near] * len(parts),
        out_specs=near,
        compiler_params=pltpu.CompilerParams(vmem_limit_bytes=GRANT),
        cost_estimate=pl.CostEstimate(
            flops=len(parts) * minutes * width,
            bytes_accessed=4 * len(parts) * minutes * width,
            transcendentals=0,
        ),
    )(*parts)


def products(left, parts, at):
    width = parts[0].shape[1]
    if width >= 2 * LANES:
        for part in parts:
            yield jnp.dot(left[at], part[...], preferred_element_type=jnp.float32)
    else:
        joined = jnp.concatenate([part[...] for part in parts], axis=1)
        result = jnp.dot(left[at], joined, preferred_element_type=jnp.float32)
        for k in range(len(parts)):
            yield result[:, k * width : (k + 1) * width]


def decayed_kernel(where, factor, prior, out, sem):
    count, _, width = out.shape
    kept, _ = decay(factor)

    def fetch(k):
        return pltpu.make_async_copy(
            prior.at[:, columns_of(where, k, width)], out.at[k], sem.at[k]
        )

    for k in range(count):
        fetch(k).start()
    for k in range(count):
        fetch(k).wait()
        out[k] = kept * out[k]


def own_kernel(where, rows, factor, *refs):
    count = len(where)
    own, left, prior, out, sem = refs[:count], *refs[count:]
    height, width = out.shape[1:]
    kept, _ = decay(factor)

    def fetch(k, i):
        at = pl.ds(i * rows, rows)
        return pltpu.make_async_copy(
            prior.at[at, columns_of(where, k, width)], out.at[k, at], sem.at[k, i]
        )

    for i in range(height // rows):
        for k in range(count):
            fetch(k, i).start()

    @pl.loop(0, height // rows)
    def _(i):
        at = pl.ds(pl.multiple_of(i * rows, rows), rows)
        for k, product in enumerate(products(left, own, at)):
            fetch(k, i).wait()
            out[k, at] = kept * out[k, at] + product


def own_late_kernel(count, rows, *refs):
    own, left, base, out = refs[:count], *refs[count:]

    @pl.loop(0, out.shape[1] // rows)
    def _(i):
        at = pl.ds(pl.multiple_of(i * rows, rows), rows)
        for k, product in enumerate(products(left, own, at)):
            out[k, at] = base[k, at] + product


def other_kernel(where, rows, factor, *refs):
    count = len(where)
    other, left, base = refs[:count], *refs[count : count + 2]
    out, box, sem = refs[-3:]
    height, width = box.shape[1:]
    _, earlier = decay(factor)

    def flush(source, k, i):
        at = pl.ds(i * rows, rows)
        return pltpu.make_async_copy(
            source.at[k, at], out.at[0, at, columns_of(where, k, width)], sem.at[k, i]
        )

    @pl.loop(0, height // rows)
    def _(i):
        at = pl.ds(pl.multiple_of(i * rows, rows), rows)

        @pl.when(earlier)
        def _():
            for k, product in enumerate(products(left, other, at)):
                box[k, at] = base[k, at] + factor * product
                flush(box, k, i).start()

        @pl.when(jnp.logical_not(earlier))
        def _():
            for k in range(count):
                flush(base, k, i).start()

    for i in range(height // rows):
        for k in range(count):
            flush(box, k, i).wait()


def tile_calls(where, own, left_own, left_other, prior, rows, factor, early):
    count = len(own)
    minutes, width = own[0].shape
    height, total = prior.shape
    tiles = height // rows
    near = pl.BlockSpec(memory_space=pltpu.VMEM)
    far = pl.BlockSpec(memory_space=pltpu.HBM)
    small = pltpu.VMEM((count, height, width), jnp.float32)
    grant = pltpu.CompilerParams(vmem_limit_bytes=GRANT)
    size = 4 * count * height * width
    flops = 2 * count * minutes * width * height

    def cost(flops, bytes_accessed):
        return pl.CostEstimate(flops=flops, bytes_accessed=bytes_accessed, transcendentals=0)

    if early:
        base = pl.pallas_call(
            functools.partial(decayed_kernel, where, factor),
            out_shape=small,
            in_specs=[far],
            out_specs=near,
            scratch_shapes=[pltpu.SemaphoreType.DMA((count,))],
            compiler_params=grant,
            cost_estimate=cost(size // 4, size),
        )(prior)
        base = pl.pallas_call(
            functools.partial(own_late_kernel, count, rows),
            out_shape=small,
            in_specs=[near] * (count + 2),
            out_specs=near,
            compiler_params=grant,
            cost_estimate=cost(flops, size),
        )(*own, left_own, base)
    else:
        base = pl.pallas_call(
            functools.partial(own_kernel, where, rows, factor),
            out_shape=small,
            in_specs=[near] * (count + 1) + [far],
            out_specs=near,
            scratch_shapes=[pltpu.SemaphoreType.DMA((count, tiles))],
            compiler_params=grant,
            cost_estimate=cost(flops, 2 * size),
        )(*own, left_own, prior)

    def finish(out, other):
        args = [*other, left_other, base]
        in_specs = [near] * (count + 2)
        aliases = {}
        if out is not None:
            aliases = {len(args): 0}
            args.append(out)
            in_specs.append(far)
        return pl.pallas_call(
            functools.partial(other_kernel, where, rows, factor),
            out_shape=pltpu.HBM((1, height, total), jnp.float32),
            in_specs=in_specs,
            out_specs=far,
            scratch_shapes=[
                pltpu.VMEM(small.shape, small.dtype),
                pltpu.SemaphoreType.DMA((count, tiles)),
            ],
            input_output_aliases=aliases,
            compiler_params=grant,
            cost_estimate=cost(flops, 2 * size),
        )(*args)

    return finish


def last_cuts(half):
    rest = [half // 2**k for k in range(1, LAST_HOPS)]
    return (*rest, rest[-1])


def local_ring(returns, prior):
    minutes, width = returns.shape
    n = lax.axis_size("assets")
    half = width // 2
    rows = min(prior.shape[0], 512)

    cycle = list(range(0, n, 2)) + list(range(n - 1, 0, -2))
    forward = [(cycle[k], cycle[(k + 1) % n]) for k in range(n)]
    backward = [(b, a) for a, b in forward]

    def swap(pieces):
        moved = []
        for part in pieces:
            moved.append(lax.ppermute(part, "tm", [(0, 1), (1, 0)]))
        return moved

    weight, factor = constants(minutes)

    def hop(parts):
        moved = []
        for way, pairs in enumerate((forward, backward)):
            moved.append(lax.ppermute(parts[way], "assets", pairs))
        return moved

    halves = split_call(returns, jnp.asarray(weight.reshape(-1, LANES)), 2)
    flight = [halves, halves[::-1]]
    arrived = []
    for k in range(n - 2):
        flight[k % 2] = hop(flight[k % 2])
        arrived.append((flight[k % 2], k // 2 + 1, (k % 2, 1 - k % 2), 0))
    start = 0
    for part in last_cuts(half):
        cut = slice(start, start + part)
        arrived.append((hop([f[:, cut] for f in flight[0]]), n // 2, (0, 1), start))
        start = start + part

    own_other = swap(halves)
    left_own = turn_call(halves)
    left_other = turn_call(own_other)

    prior = in_hbm(prior)
    common = (left_own, left_other, prior, rows, factor)
    where = tuple((0, width, k * half) for k in (0, 1))
    out = tile_calls(where, halves, *common, False)(None, own_other)
    for k, (pair, step, sides, start) in enumerate(arrived):
        where = tuple(
            (way_step, width, side * half + start)
            for way_step, side in zip((step, -step), sides, strict=True)
        )
        finish = tile_calls(where, pair, *common, k >= n - 2)
        out = finish(out, swap(pair))
    return out


def solution(mesh):
    n, slabs = mesh.shape["assets"], mesh.shape["tm"]

    def rings(minutes, width):
        even = slabs == 2 and n % 2 == 0 and 4 <= n <= 16
        return even and minutes % LANES == 0 and width % (8 * LANES) == 0

    def local(returns, prior):
        if not rings(*returns.shape):
            return local_any(returns, prior)
        return local_ring(returns, prior)

    placed = (P("tm", ("groups", "assets")), P(("groups", "assets"), None))
    return jax.shard_map(
        local,
        mesh=mesh,
        in_specs=placed,
        out_specs=P("tm", ("groups", "assets"), None),
        check_vma=False,
    )
```

```python
import functools

import jax
import jax.numpy as jnp
import numpy as np
from jax import lax
from jax.experimental import pallas as pl
from jax.experimental.pallas import tpu as pltpu
from jax.sharding import PartitionSpec as P


LANES = 128
GRANT = 16 * 2**20
LAST_HOPS = 2


def weights(minutes):
    lam = jnp.float32(0.9995)
    position = jnp.arange(minutes, dtype=jnp.float32)
    weight = jnp.sqrt(
        (jnp.float32(1.0) - lam) * jnp.power(lam, jnp.float32(minutes - 1) - position)
    )
    return weight, jnp.power(lam, jnp.float32(minutes))


def constants(minutes):
    lam = np.float32(0.9995)
    position = np.arange(minutes, dtype=np.float32)
    weight = np.sqrt(
        (np.float32(1.0) - lam) * np.power(lam, np.float32(minutes - 1) - position)
    )
    return weight.astype(np.float32), np.power(lam, np.float32(minutes))


def scale(part, weight):
    return (part.astype(jnp.float32) * weight[:, None]).astype(jnp.bfloat16)


def prefix(shard, axis, combine, identity):
    length, mine = (lax.axis_size(axis), lax.axis_index(axis))
    everything = jax.tree.map(
        lambda part: lax.all_gather(part.astype(jnp.bfloat16), axis), shard
    )
    start = jax.tree.map(
        lambda part, zero: jnp.broadcast_to(jnp.asarray(zero, part.dtype), part.shape),
        shard,
        identity,
    )

    def turn(k, before):
        reached = k < mine
        new = combine(
            before, jax.tree.map(lambda part, own: part[k].astype(own.dtype), everything, shard)
        )
        return jax.tree.map(lambda a, b: jnp.where(reached, a, b), new, before)

    return lax.fori_loop(0, length, turn, start)


def combine_carry(earlier, later):
    return (later[1] * earlier[0] + later[0], earlier[1] * later[1])


def local_any(returns, prior):
    weight, factor = weights(returns.shape[0])
    scaled = scale(returns, weight)
    tile = lax.dot_general(
        scaled,
        lax.all_gather(scaled, "assets", axis=1, tiled=True),
        (((0,), (0,)), ((), ())),
        preferred_element_type=jnp.float32,
    )
    decay = jnp.full((1,), factor, jnp.float32)
    identity = (jnp.zeros_like(tile), jnp.ones((1,), jnp.float32))
    before, reach = prefix((tile, decay), "tm", combine_carry, identity)
    return (factor * (before + reach[0] * prior) + tile)[None]


def owner(step):
    n, me = lax.axis_size("assets"), lax.axis_index("assets")
    place = jnp.where(me % 2 == 0, me // 2, n - 1 - me // 2)
    at = lax.rem(place - step + 2 * n, n)
    return jnp.where(at < n // 2, 2 * at, 2 * (n - 1 - at) + 1)


def columns_of(where, k, width):
    step, block, offset = where[k]
    return pl.ds(pl.multiple_of(owner(step) * block + offset, LANES), width)


def decay(factor):
    first = lax.axis_index("tm") == 0
    return jnp.where(first, factor, factor * factor), jnp.logical_not(first)


def in_hbm(x):
    return pltpu.with_memory_space_constraint(x, pltpu.HBM)


def split_kernel(returns, weight, *refs):
    parts, (box, row, wide, sem, row_sem) = refs[:-5], refs[-5:]
    width = parts[0].shape[1]
    copies = []
    row_copy = pltpu.make_async_copy(weight, row, row_sem)
    row_copy.start()
    rows = returns.shape[0] // sem.shape[0]
    for k in range(sem.shape[0]):
        at = slice(k * rows, (k + 1) * rows)
        copies.append(pltpu.make_async_copy(returns.at[at], box.at[at], sem.at[k]))
        copies[-1].start()
    row_copy.wait()
    for k in range(row.shape[0]):
        wide[k * LANES : (k + 1) * LANES, :] = jnp.broadcast_to(
            row[k : k + 1, :], (LANES, LANES)
        ).T
    for k, copy in enumerate(copies):
        copy.wait()
        at = slice(k * rows, (k + 1) * rows)
        for lane in range(0, returns.shape[1], LANES):
            part, start = parts[lane // width], lane % width
            part[at, start : start + LANES] = (
                box[at, lane : lane + LANES].astype(jnp.float32) * wide[at]
            ).astype(jnp.bfloat16)


def split_call(returns, weight, count):
    minutes, width = returns.shape
    near = pl.BlockSpec(memory_space=pltpu.VMEM)
    part = pltpu.VMEM((minutes, width // count), jnp.bfloat16)
    return pl.pallas_call(
        split_kernel,
        out_shape=[part] * count,
        in_specs=[pl.BlockSpec(memory_space=pltpu.HBM)] * 2,
        out_specs=[near] * count,
        scratch_shapes=[
            pltpu.VMEM((minutes, width), jnp.bfloat16),
            pltpu.VMEM(weight.shape, weight.dtype),
            pltpu.VMEM((minutes, LANES), jnp.float32),
            pltpu.SemaphoreType.DMA((max(1, minutes // (2 * LANES)),)),
            pltpu.SemaphoreType.DMA,
        ],
        compiler_params=pltpu.CompilerParams(vmem_limit_bytes=GRANT),
        cost_estimate=pl.CostEstimate(
            flops=minutes * width, bytes_accessed=4 * minutes * width, transcendentals=0
        ),
    )(in_hbm(returns), in_hbm(weight))


def turn_kernel(*refs):
    parts, out = refs[:-1], refs[-1]
    width = parts[0].shape[1]
    for k, part in enumerate(parts):
        for lane in range(0, width, LANES):
            at = slice(k * width + lane, k * width + lane + LANES)
            out[at, :] = part[:, lane : lane + LANES].T


def turn_call(parts):
    minutes, width = parts[0].shape
    near = pl.BlockSpec(memory_space=pltpu.VMEM)
    return pl.pallas_call(
        turn_kernel,
        out_shape=pltpu.VMEM((len(parts) * width, minutes), jnp.bfloat16),
        in_specs=[near] * len(parts),
        out_specs=near,
        compiler_params=pltpu.CompilerParams(vmem_limit_bytes=GRANT),
        cost_estimate=pl.CostEstimate(
            flops=len(parts) * minutes * width,
            bytes_accessed=4 * len(parts) * minutes * width,
            transcendentals=0,
        ),
    )(*parts)


def products(left, parts, at):
    width = parts[0].shape[1]
    if width >= 2 * LANES:
        for part in parts:
            yield jnp.dot(left[at], part[...], preferred_element_type=jnp.float32)
    else:
        joined = jnp.concatenate([part[...] for part in parts], axis=1)
        result = jnp.dot(left[at], joined, preferred_element_type=jnp.float32)
        for k in range(len(parts)):
            yield result[:, k * width : (k + 1) * width]


def decayed_kernel(where, factor, prior, out, sem):
    count, _, width = out.shape
    kept, _ = decay(factor)

    def fetch(k):
        return pltpu.make_async_copy(
            prior.at[:, columns_of(where, k, width)], out.at[k], sem.at[k]
        )

    for k in range(count):
        fetch(k).start()
    for k in range(count):
        fetch(k).wait()
        out[k] = kept * out[k]


def own_kernel(where, rows, factor, *refs):
    count = len(where)
    own, left, prior, out, sem = refs[:count], *refs[count:]
    height, width = out.shape[1:]
    kept, _ = decay(factor)

    def fetch(k, i):
        at = pl.ds(i * rows, rows)
        return pltpu.make_async_copy(
            prior.at[at, columns_of(where, k, width)], out.at[k, at], sem.at[k, i]
        )

    for i in range(height // rows):
        for k in range(count):
            fetch(k, i).start()

    @pl.loop(0, height // rows)
    def _(i):
        at = pl.ds(pl.multiple_of(i * rows, rows), rows)
        for k, product in enumerate(products(left, own, at)):
            fetch(k, i).wait()
            out[k, at] = kept * out[k, at] + product


def own_late_kernel(count, rows, *refs):
    own, left, base, out = refs[:count], *refs[count:]

    @pl.loop(0, out.shape[1] // rows)
    def _(i):
        at = pl.ds(pl.multiple_of(i * rows, rows), rows)
        for k, product in enumerate(products(left, own, at)):
            out[k, at] = base[k, at] + product


def other_kernel(where, rows, factor, *refs):
    count = len(where)
    other, left, base = refs[:count], *refs[count : count + 2]
    out, box, sem = refs[-3:]
    height, width = box.shape[1:]
    _, earlier = decay(factor)

    def flush(source, k, i):
        at = pl.ds(i * rows, rows)
        return pltpu.make_async_copy(
            source.at[k, at], out.at[0, at, columns_of(where, k, width)], sem.at[k, i]
        )

    @pl.loop(0, height // rows)
    def _(i):
        at = pl.ds(pl.multiple_of(i * rows, rows), rows)

        @pl.when(earlier)
        def _():
            for k, product in enumerate(products(left, other, at)):
                box[k, at] = base[k, at] + factor * product
                flush(box, k, i).start()

        @pl.when(jnp.logical_not(earlier))
        def _():
            for k in range(count):
                flush(base, k, i).start()

    for i in range(height // rows):
        for k in range(count):
            flush(box, k, i).wait()


def tile_calls(where, own, left_own, left_other, prior, rows, factor, early):
    count = len(own)
    minutes, width = own[0].shape
    height, total = prior.shape
    tiles = height // rows
    near = pl.BlockSpec(memory_space=pltpu.VMEM)
    far = pl.BlockSpec(memory_space=pltpu.HBM)
    small = pltpu.VMEM((count, height, width), jnp.float32)
    grant = pltpu.CompilerParams(vmem_limit_bytes=GRANT)
    size = 4 * count * height * width
    flops = 2 * count * minutes * width * height

    def cost(flops, bytes_accessed):
        return pl.CostEstimate(flops=flops, bytes_accessed=bytes_accessed, transcendentals=0)

    if early:
        base = pl.pallas_call(
            functools.partial(decayed_kernel, where, factor),
            out_shape=small,
            in_specs=[far],
            out_specs=near,
            scratch_shapes=[pltpu.SemaphoreType.DMA((count,))],
            compiler_params=grant,
            cost_estimate=cost(size // 4, size),
        )(prior)
        base = pl.pallas_call(
            functools.partial(own_late_kernel, count, rows),
            out_shape=small,
            in_specs=[near] * (count + 2),
            out_specs=near,
            compiler_params=grant,
            cost_estimate=cost(flops, size),
        )(*own, left_own, base)
    else:
        base = pl.pallas_call(
            functools.partial(own_kernel, where, rows, factor),
            out_shape=small,
            in_specs=[near] * (count + 1) + [far],
            out_specs=near,
            scratch_shapes=[pltpu.SemaphoreType.DMA((count, tiles))],
            compiler_params=grant,
            cost_estimate=cost(flops, 2 * size),
        )(*own, left_own, prior)

    def finish(out, other):
        args = [*other, left_other, base]
        in_specs = [near] * (count + 2)
        aliases = {}
        if out is not None:
            aliases = {len(args): 0}
            args.append(out)
            in_specs.append(far)
        return pl.pallas_call(
            functools.partial(other_kernel, where, rows, factor),
            out_shape=pltpu.HBM((1, height, total), jnp.float32),
            in_specs=in_specs,
            out_specs=far,
            scratch_shapes=[
                pltpu.VMEM(small.shape, small.dtype),
                pltpu.SemaphoreType.DMA((count, tiles)),
            ],
            input_output_aliases=aliases,
            compiler_params=grant,
            cost_estimate=cost(flops, 2 * size),
        )(*args)

    return finish


def early_kernel(count, rows, factor, *refs):
    other, left, base, out = refs[:count], *refs[count:]
    _, earlier = decay(factor)

    @pl.loop(0, out.shape[1] // rows)
    def _(i):
        at = pl.ds(pl.multiple_of(i * rows, rows), rows)

        @pl.when(earlier)
        def _():
            for k, product in enumerate(products(left, other, at)):
                out[k, at] = base[k, at] + factor * product

        @pl.when(jnp.logical_not(earlier))
        def _():
            for k in range(count):
                out[k, at] = base[k, at]


def final_kernel(where, rows, factor, *refs):
    count = len(where)
    choices = refs[:count], refs[count : 2 * count]
    left, base = refs[2 * count : 2 * count + 2]
    out, box, sem = refs[-3:]
    height, width = box.shape[1:]
    _, earlier = decay(factor)

    def flush(k, i):
        at = pl.ds(i * rows, rows)
        return pltpu.make_async_copy(
            box.at[k, at], out.at[0, at, columns_of(where, k, width)], sem.at[k, i]
        )

    @pl.loop(0, height // rows)
    def _(i):
        at = pl.ds(pl.multiple_of(i * rows, rows), rows)
        for own, mine in zip(choices, (jnp.logical_not(earlier), earlier), strict=True):

            @pl.when(mine)
            def _():
                for k, product in enumerate(products(left, own, at)):
                    box[k, at] = base[k, at] + product
                    flush(k, i).start()

    for i in range(height // rows):
        for k in range(count):
            flush(k, i).wait()


def last_calls(where, left_own, left_other, prior, rows, factor):
    count = len(where)
    height, total = prior.shape
    near = pl.BlockSpec(memory_space=pltpu.VMEM)
    far = pl.BlockSpec(memory_space=pltpu.HBM)
    grant = pltpu.CompilerParams(vmem_limit_bytes=GRANT)
    width = total // lax.axis_size("assets") // 2 // LAST_HOPS
    small = pltpu.VMEM((count, height, width), jnp.float32)
    size = 4 * count * height * width
    flops = 2 * count * left_own.shape[1] * width * height

    def cost(flops, bytes_accessed):
        return pl.CostEstimate(flops=flops, bytes_accessed=bytes_accessed, transcendentals=0)

    base = pl.pallas_call(
        functools.partial(decayed_kernel, where, factor),
        out_shape=small,
        in_specs=[far],
        out_specs=near,
        scratch_shapes=[pltpu.SemaphoreType.DMA((count,))],
        compiler_params=grant,
        cost_estimate=cost(size // 4, size),
    )(prior)

    def early(other):
        return pl.pallas_call(
            functools.partial(early_kernel, count, rows, factor),
            out_shape=small,
            in_specs=[near] * (count + 2),
            out_specs=near,
            compiler_params=grant,
            cost_estimate=cost(flops, size),
        )(*other, left_other, base)

    def final(out, first, second, base):
        args = [*first, *second, left_own, base, out]
        return pl.pallas_call(
            functools.partial(final_kernel, where, rows, factor),
            out_shape=pltpu.HBM(out.shape, out.dtype),
            in_specs=[near] * (2 * count + 2) + [far],
            out_specs=far,
            scratch_shapes=[
                pltpu.VMEM(small.shape, small.dtype),
                pltpu.SemaphoreType.DMA((count, height // rows)),
            ],
            input_output_aliases={len(args) - 1: 0},
            compiler_params=grant,
            cost_estimate=cost(flops, 2 * size),
        )(*args)

    return early, final


def local_ring(returns, prior):
    minutes, width = returns.shape
    n = lax.axis_size("assets")
    half = width // 2
    rows = min(prior.shape[0], 512)

    cycle = list(range(0, n, 2)) + list(range(n - 1, 0, -2))
    forward = [(cycle[k], cycle[(k + 1) % n]) for k in range(n)]
    backward = [(b, a) for a, b in forward]

    def swap(pieces):
        moved = []
        for part in pieces:
            moved.append(lax.ppermute(part, "tm", [(0, 1), (1, 0)]))
        return moved

    weight, factor = constants(minutes)

    def hop(parts):
        moved = []
        for way, pairs in enumerate((forward, backward)):
            moved.append(lax.ppermute(parts[way], "assets", pairs))
        return moved

    halves = split_call(returns, jnp.asarray(weight.reshape(-1, LANES)), 2)
    flight = [halves, halves[::-1]]
    arrived = []
    for k in range(n - 2):
        flight[k % 2] = hop(flight[k % 2])
        arrived.append((flight[k % 2], k // 2 + 1, (k % 2, 1 - k % 2), 0))
    cut = half // LAST_HOPS
    parts = [f[:, :cut] for f in flight[0]]
    arrived.append((hop(parts), n // 2, (0, 1), 0))

    own_other = swap(halves)
    left_own = turn_call(halves)
    left_other = turn_call(own_other)

    prior = in_hbm(prior)
    common = (left_own, left_other, prior, rows, factor)
    where = tuple((0, width, k * half) for k in (0, 1))
    out = tile_calls(where, halves, *common, False)(None, own_other)
    for k, (pair, step, sides, start) in enumerate(arrived):
        where = tuple(
            (way_step, width, side * half + start)
            for way_step, side in zip((step, -step), sides, strict=True)
        )
        finish = tile_calls(where, pair, *common, k >= n - 2)
        other = swap(pair)
        if k == n - 4:
            crossed = [part[:, cut:] for part in other]
        out = finish(out, other)

    both = ("assets", "tm")
    direct = {"p": [], "q": []}
    for way, pairs in enumerate((forward, backward)):
        for name, sender in (("p", 1), ("q", 0)):
            links = [(2 * a + sender, 2 * b + 1) for a, b in pairs]
            direct[name].append(lax.ppermute(crossed[way], both, links))
    handed = []
    for part in direct["p"]:
        handed.append(lax.ppermute(part, "tm", [(0, 1), (1, 0)]))
    where = tuple((s, width, side * half + cut) for s, side in ((n // 2, 0), (-(n // 2), 1)))
    early, final = last_calls(where, *common)
    return final(out, handed, direct["q"], early(direct["p"]))


def solution(mesh):
    n, slabs = mesh.shape["assets"], mesh.shape["tm"]

    def rings(minutes, width):
        even = slabs == 2 and n % 2 == 0 and 4 <= n <= 16
        return even and minutes % LANES == 0 and width % (8 * LANES) == 0

    def local(returns, prior):
        if not rings(*returns.shape):
            return local_any(returns, prior)
        return local_ring(returns, prior)

    placed = (P("tm", ("groups", "assets")), P(("groups", "assets"), None))
    return jax.shard_map(
        local,
        mesh=mesh,
        in_specs=placed,
        out_specs=P("tm", ("groups", "assets"), None),
        check_vma=False,
    )
```

```python
import functools

import jax
import jax.numpy as jnp
import numpy as np
from jax import lax
from jax.experimental import pallas as pl
from jax.experimental.pallas import tpu as pltpu
from jax.sharding import PartitionSpec as P


LANES = 128
GRANT = 16 * 2**20
LAST_HOPS = 2


def weights(minutes):
    lam = jnp.float32(0.9995)
    position = jnp.arange(minutes, dtype=jnp.float32)
    weight = jnp.sqrt(
        (jnp.float32(1.0) - lam) * jnp.power(lam, jnp.float32(minutes - 1) - position)
    )
    return weight, jnp.power(lam, jnp.float32(minutes))


def constants(minutes):
    lam = np.float32(0.9995)
    position = np.arange(minutes, dtype=np.float32)
    weight = np.sqrt(
        (np.float32(1.0) - lam) * np.power(lam, np.float32(minutes - 1) - position)
    )
    return weight.astype(np.float32), np.power(lam, np.float32(minutes))


def scale(part, weight):
    return (part.astype(jnp.float32) * weight[:, None]).astype(jnp.bfloat16)


def prefix(shard, axis, combine, identity):
    length, mine = (lax.axis_size(axis), lax.axis_index(axis))
    everything = jax.tree.map(
        lambda part: lax.all_gather(part.astype(jnp.bfloat16), axis), shard
    )
    start = jax.tree.map(
        lambda part, zero: jnp.broadcast_to(jnp.asarray(zero, part.dtype), part.shape),
        shard,
        identity,
    )

    def turn(k, before):
        reached = k < mine
        new = combine(
            before, jax.tree.map(lambda part, own: part[k].astype(own.dtype), everything, shard)
        )
        return jax.tree.map(lambda a, b: jnp.where(reached, a, b), new, before)

    return lax.fori_loop(0, length, turn, start)


def combine_carry(earlier, later):
    return (later[1] * earlier[0] + later[0], earlier[1] * later[1])


def local_any(returns, prior):
    weight, factor = weights(returns.shape[0])
    scaled = scale(returns, weight)
    tile = lax.dot_general(
        scaled,
        lax.all_gather(scaled, "assets", axis=1, tiled=True),
        (((0,), (0,)), ((), ())),
        preferred_element_type=jnp.float32,
    )
    decay = jnp.full((1,), factor, jnp.float32)
    identity = (jnp.zeros_like(tile), jnp.ones((1,), jnp.float32))
    before, reach = prefix((tile, decay), "tm", combine_carry, identity)
    return (factor * (before + reach[0] * prior) + tile)[None]


def owner(step):
    n, me = lax.axis_size("assets"), lax.axis_index("assets")
    place = jnp.where(me % 2 == 0, me // 2, n - 1 - me // 2)
    at = lax.rem(place - step + 2 * n, n)
    return jnp.where(at < n // 2, 2 * at, 2 * (n - 1 - at) + 1)


def columns_of(where, k, width):
    step, block, offset = where[k]
    return pl.ds(pl.multiple_of(owner(step) * block + offset, LANES), width)


def decay(factor):
    first = lax.axis_index("tm") == 0
    return jnp.where(first, factor, factor * factor), jnp.logical_not(first)


def in_hbm(x):
    return pltpu.with_memory_space_constraint(x, pltpu.HBM)


def split_kernel(returns, weight, *refs):
    parts, (box, row, wide, sem, row_sem) = refs[:-5], refs[-5:]
    width = parts[0].shape[1]
    copies = []
    row_copy = pltpu.make_async_copy(weight, row, row_sem)
    row_copy.start()
    rows = returns.shape[0] // sem.shape[0]
    for k in range(sem.shape[0]):
        at = slice(k * rows, (k + 1) * rows)
        copies.append(pltpu.make_async_copy(returns.at[at], box.at[at], sem.at[k]))
        copies[-1].start()
    row_copy.wait()
    for k in range(row.shape[0]):
        wide[k * LANES : (k + 1) * LANES, :] = jnp.broadcast_to(
            row[k : k + 1, :], (LANES, LANES)
        ).T
    for k, copy in enumerate(copies):
        copy.wait()
        at = slice(k * rows, (k + 1) * rows)
        for lane in range(0, returns.shape[1], LANES):
            part, start = parts[lane // width], lane % width
            part[at, start : start + LANES] = (
                box[at, lane : lane + LANES].astype(jnp.float32) * wide[at]
            ).astype(jnp.bfloat16)


def split_call(returns, weight, count):
    minutes, width = returns.shape
    near = pl.BlockSpec(memory_space=pltpu.VMEM)
    part = pltpu.VMEM((minutes, width // count), jnp.bfloat16)
    return pl.pallas_call(
        split_kernel,
        out_shape=[part] * count,
        in_specs=[pl.BlockSpec(memory_space=pltpu.HBM)] * 2,
        out_specs=[near] * count,
        scratch_shapes=[
            pltpu.VMEM((minutes, width), jnp.bfloat16),
            pltpu.VMEM(weight.shape, weight.dtype),
            pltpu.VMEM((minutes, LANES), jnp.float32),
            pltpu.SemaphoreType.DMA((max(1, minutes // (2 * LANES)),)),
            pltpu.SemaphoreType.DMA,
        ],
        compiler_params=pltpu.CompilerParams(vmem_limit_bytes=GRANT),
        cost_estimate=pl.CostEstimate(
            flops=minutes * width, bytes_accessed=4 * minutes * width, transcendentals=0
        ),
    )(in_hbm(returns), in_hbm(weight))


def turn_kernel(*refs):
    parts, out = refs[:-1], refs[-1]
    width = parts[0].shape[1]
    for k, part in enumerate(parts):
        for lane in range(0, width, LANES):
            at = slice(k * width + lane, k * width + lane + LANES)
            out[at, :] = part[:, lane : lane + LANES].T


def turn_call(parts):
    minutes, width = parts[0].shape
    near = pl.BlockSpec(memory_space=pltpu.VMEM)
    return pl.pallas_call(
        turn_kernel,
        out_shape=pltpu.VMEM((len(parts) * width, minutes), jnp.bfloat16),
        in_specs=[near] * len(parts),
        out_specs=near,
        compiler_params=pltpu.CompilerParams(vmem_limit_bytes=GRANT),
        cost_estimate=pl.CostEstimate(
            flops=len(parts) * minutes * width,
            bytes_accessed=4 * len(parts) * minutes * width,
            transcendentals=0,
        ),
    )(*parts)


def products(left, parts, at):
    width = parts[0].shape[1]
    if width >= 2 * LANES:
        for part in parts:
            yield jnp.dot(left[at], part[...], preferred_element_type=jnp.float32)
    else:
        joined = jnp.concatenate([part[...] for part in parts], axis=1)
        result = jnp.dot(left[at], joined, preferred_element_type=jnp.float32)
        for k in range(len(parts)):
            yield result[:, k * width : (k + 1) * width]


def decayed_kernel(where, factor, prior, out, sem):
    count, _, width = out.shape
    kept, _ = decay(factor)

    def fetch(k):
        return pltpu.make_async_copy(
            prior.at[:, columns_of(where, k, width)], out.at[k], sem.at[k]
        )

    for k in range(count):
        fetch(k).start()
    for k in range(count):
        fetch(k).wait()
        out[k] = kept * out[k]


def own_kernel(where, rows, factor, *refs):
    count = len(where)
    own, left, prior, out, sem = refs[:count], *refs[count:]
    height, width = out.shape[1:]
    kept, _ = decay(factor)

    def fetch(k, i):
        at = pl.ds(i * rows, rows)
        return pltpu.make_async_copy(
            prior.at[at, columns_of(where, k, width)], out.at[k, at], sem.at[k, i]
        )

    for i in range(height // rows):
        for k in range(count):
            fetch(k, i).start()

    @pl.loop(0, height // rows)
    def _(i):
        at = pl.ds(pl.multiple_of(i * rows, rows), rows)
        for k, product in enumerate(products(left, own, at)):
            fetch(k, i).wait()
            out[k, at] = kept * out[k, at] + product


def own_late_kernel(count, rows, *refs):
    own, left, base, out = refs[:count], *refs[count:]

    @pl.loop(0, out.shape[1] // rows)
    def _(i):
        at = pl.ds(pl.multiple_of(i * rows, rows), rows)
        for k, product in enumerate(products(left, own, at)):
            out[k, at] = base[k, at] + product


def other_kernel(where, rows, factor, *refs):
    count = len(where)
    other, left, base = refs[:count], *refs[count : count + 2]
    out, box, sem = refs[-3:]
    height, width = box.shape[1:]
    _, earlier = decay(factor)

    def flush(source, k, i):
        at = pl.ds(i * rows, rows)
        return pltpu.make_async_copy(
            source.at[k, at], out.at[0, at, columns_of(where, k, width)], sem.at[k, i]
        )

    @pl.loop(0, height // rows)
    def _(i):
        at = pl.ds(pl.multiple_of(i * rows, rows), rows)

        @pl.when(earlier)
        def _():
            for k, product in enumerate(products(left, other, at)):
                box[k, at] = base[k, at] + factor * product
                flush(box, k, i).start()

        @pl.when(jnp.logical_not(earlier))
        def _():
            for k in range(count):
                flush(base, k, i).start()

    for i in range(height // rows):
        for k in range(count):
            flush(box, k, i).wait()


def tile_calls(where, own, left_own, left_other, prior, rows, factor, early):
    count = len(own)
    minutes, width = own[0].shape
    height, total = prior.shape
    tiles = height // rows
    near = pl.BlockSpec(memory_space=pltpu.VMEM)
    far = pl.BlockSpec(memory_space=pltpu.HBM)
    small = pltpu.VMEM((count, height, width), jnp.float32)
    grant = pltpu.CompilerParams(vmem_limit_bytes=GRANT)
    size = 4 * count * height * width
    flops = 2 * count * minutes * width * height

    def cost(flops, bytes_accessed):
        return pl.CostEstimate(flops=flops, bytes_accessed=bytes_accessed, transcendentals=0)

    if early:
        base = pl.pallas_call(
            functools.partial(decayed_kernel, where, factor),
            out_shape=small,
            in_specs=[far],
            out_specs=near,
            scratch_shapes=[pltpu.SemaphoreType.DMA((count,))],
            compiler_params=grant,
            cost_estimate=cost(size // 4, size),
        )(prior)
        base = pl.pallas_call(
            functools.partial(own_late_kernel, count, rows),
            out_shape=small,
            in_specs=[near] * (count + 2),
            out_specs=near,
            compiler_params=grant,
            cost_estimate=cost(flops, size),
        )(*own, left_own, base)
    else:
        base = pl.pallas_call(
            functools.partial(own_kernel, where, rows, factor),
            out_shape=small,
            in_specs=[near] * (count + 1) + [far],
            out_specs=near,
            scratch_shapes=[pltpu.SemaphoreType.DMA((count, tiles))],
            compiler_params=grant,
            cost_estimate=cost(flops, 2 * size),
        )(*own, left_own, prior)

    def finish(out, other):
        args = [*other, left_other, base]
        in_specs = [near] * (count + 2)
        aliases = {}
        if out is not None:
            aliases = {len(args): 0}
            args.append(out)
            in_specs.append(far)
        return pl.pallas_call(
            functools.partial(other_kernel, where, rows, factor),
            out_shape=pltpu.HBM((1, height, total), jnp.float32),
            in_specs=in_specs,
            out_specs=far,
            scratch_shapes=[
                pltpu.VMEM(small.shape, small.dtype),
                pltpu.SemaphoreType.DMA((count, tiles)),
            ],
            input_output_aliases=aliases,
            compiler_params=grant,
            cost_estimate=cost(flops, 2 * size),
        )(*args)

    return finish


def pick_kernel(first, second, out):
    for source, mine in ((first, 0), (second, 1)):

        @pl.when(lax.axis_index("tm") == mine)
        def _():
            out[...] = source[...]


def pick_call(first, second):
    near = pl.BlockSpec(memory_space=pltpu.VMEM)
    return pl.pallas_call(
        pick_kernel,
        out_shape=pltpu.VMEM(first.shape, first.dtype),
        in_specs=[near] * 2,
        out_specs=near,
        compiler_params=pltpu.CompilerParams(vmem_limit_bytes=GRANT),
        cost_estimate=pl.CostEstimate(
            flops=0, bytes_accessed=4 * first.size, transcendentals=0
        ),
    )(first, second)


def early_kernel(rows, factor, mixed, straight, left_own, left_other, base, out):
    _, earlier = decay(factor)

    @pl.loop(0, out.shape[1] // rows)
    def _(i):
        at = pl.ds(pl.multiple_of(i * rows, rows), rows)

        def times(left, part):
            return jnp.dot(left[at], part[...], preferred_element_type=jnp.float32)

        @pl.when(earlier)
        def _():
            out[0, at] = base[0, at] + times(left_own, straight)
            out[1, at] = base[1, at] + factor * times(left_other, mixed)

        @pl.when(jnp.logical_not(earlier))
        def _():
            out[0, at] = base[0, at] + times(left_own, mixed)
            out[1, at] = base[1, at]


def final_kernel(where, rows, factor, handed, straight, left_own, left_other, base, _, *refs):
    out, box, sem = refs
    height, width = box.shape[1:]
    count, (_, earlier) = len(where), decay(factor)

    def flush(source, k, i):
        at = pl.ds(i * rows, rows)
        return pltpu.make_async_copy(
            source.at[k, at], out.at[0, at, columns_of(where, k, width)], sem.at[k, i]
        )

    @pl.loop(0, height // rows)
    def _(i):
        at = pl.ds(pl.multiple_of(i * rows, rows), rows)

        def times(left, part):
            return jnp.dot(left[at], part[...], preferred_element_type=jnp.float32)

        @pl.when(earlier)
        def _():
            box[0, at] = base[0, at] + factor * times(left_other, handed)
            flush(box, 0, i).start()
            box[1, at] = base[1, at] + times(left_own, straight)
            flush(box, 1, i).start()

        @pl.when(jnp.logical_not(earlier))
        def _():
            flush(base, 0, i).start()
            box[1, at] = base[1, at] + times(left_own, handed)
            flush(box, 1, i).start()

    for i in range(height // rows):
        for k in range(count):
            flush(box, k, i).wait()


def last_calls(where, left_own, left_other, prior, rows, factor):
    count = len(where)
    height, total = prior.shape
    near = pl.BlockSpec(memory_space=pltpu.VMEM)
    far = pl.BlockSpec(memory_space=pltpu.HBM)
    grant = pltpu.CompilerParams(vmem_limit_bytes=GRANT)
    width = total // lax.axis_size("assets") // 2 // LAST_HOPS
    small = pltpu.VMEM((count, height, width), jnp.float32)
    size = 4 * count * height * width
    flops = 2 * count * left_own.shape[1] * width * height

    def cost(flops, bytes_accessed):
        return pl.CostEstimate(flops=flops, bytes_accessed=bytes_accessed, transcendentals=0)

    base = pl.pallas_call(
        functools.partial(decayed_kernel, where, factor),
        out_shape=small,
        in_specs=[far],
        out_specs=near,
        scratch_shapes=[pltpu.SemaphoreType.DMA((count,))],
        compiler_params=grant,
        cost_estimate=cost(size // 4, size),
    )(prior)

    def early(mixed, straight):
        args = [mixed, straight, left_own, left_other, base]
        return pl.pallas_call(
            functools.partial(early_kernel, rows, factor),
            out_shape=small,
            in_specs=[near] * len(args),
            out_specs=near,
            compiler_params=grant,
            cost_estimate=cost(flops, size),
        )(*args)

    def final(out, handed, straight, base):
        args = [handed, straight, left_own, left_other, base, out]
        return pl.pallas_call(
            functools.partial(final_kernel, where, rows, factor),
            out_shape=pltpu.HBM(out.shape, out.dtype),
            in_specs=[near] * (len(args) - 1) + [far],
            out_specs=far,
            scratch_shapes=[
                pltpu.VMEM(small.shape, small.dtype),
                pltpu.SemaphoreType.DMA((count, height // rows)),
            ],
            input_output_aliases={len(args) - 1: 0},
            compiler_params=grant,
            cost_estimate=cost(flops, 2 * size),
        )(*args)

    return early, final


def local_ring(returns, prior):
    minutes, width = returns.shape
    n = lax.axis_size("assets")
    half = width // 2
    rows = min(prior.shape[0], 512)

    cycle = list(range(0, n, 2)) + list(range(n - 1, 0, -2))
    forward = [(cycle[k], cycle[(k + 1) % n]) for k in range(n)]
    backward = [(b, a) for a, b in forward]

    def swap(pieces):
        moved = []
        for part in pieces:
            moved.append(lax.ppermute(part, "tm", [(0, 1), (1, 0)]))
        return moved

    weight, factor = constants(minutes)

    def hop(parts):
        moved = []
        for way, pairs in enumerate((forward, backward)):
            moved.append(lax.ppermute(parts[way], "assets", pairs))
        return moved

    halves = split_call(returns, jnp.asarray(weight.reshape(-1, LANES)), 2)
    flight = [halves, halves[::-1]]
    arrived = []
    for k in range(n - 2):
        flight[k % 2] = hop(flight[k % 2])
        arrived.append((flight[k % 2], k // 2 + 1, (k % 2, 1 - k % 2), 0))
    cut = half // LAST_HOPS
    parts = [f[:, :cut] for f in flight[0]]
    arrived.append((hop(parts), n // 2, (0, 1), 0))

    own_other = swap(halves)
    left_own = turn_call(halves)
    left_other = turn_call(own_other)

    prior = in_hbm(prior)
    common = (left_own, left_other, prior, rows, factor)
    where = tuple((0, width, k * half) for k in (0, 1))
    out = tile_calls(where, halves, *common, False)(None, own_other)
    for k, (pair, step, sides, start) in enumerate(arrived):
        where = tuple(
            (way_step, width, side * half + start)
            for way_step, side in zip((step, -step), sides, strict=True)
        )
        finish = tile_calls(where, pair, *common, k >= n - 2)
        other = swap(pair)
        if k == n - 4:
            crossed = [part[:, cut:] for part in other]
        out = finish(out, other)

    both = ("assets", "tm")
    plain = [f[:, cut:] for f in flight[0]]
    mixed = pick_call(plain[0], crossed[1])
    links = [(2 * a, 2 * b) for a, b in forward] + [(2 * a + 1, 2 * b + 1) for a, b in backward]
    mixed = lax.ppermute(mixed, both, links)
    ahead = lax.ppermute(plain[0], both, [(2 * a + 1, 2 * b + 1) for a, b in forward])
    astern = lax.ppermute(crossed[1], both, [(2 * a, 2 * b + 1) for a, b in backward])
    handed = swap([mixed])[0]
    where = tuple((s, width, side * half + cut) for s, side in ((n // 2, 0), (-(n // 2), 1)))
    early, final = last_calls(where, *common)
    return final(out, handed, astern, early(mixed, ahead))


def solution(mesh):
    n, slabs = mesh.shape["assets"], mesh.shape["tm"]

    def rings(minutes, width):
        even = slabs == 2 and n % 2 == 0 and 4 <= n <= 16
        return even and minutes % LANES == 0 and width % (8 * LANES) == 0

    def local(returns, prior):
        if not rings(*returns.shape):
            return local_any(returns, prior)
        return local_ring(returns, prior)

    placed = (P("tm", ("groups", "assets")), P(("groups", "assets"), None))
    return jax.shard_map(
        local,
        mesh=mesh,
        in_specs=placed,
        out_specs=P("tm", ("groups", "assets"), None),
        check_vma=False,
    )
```
